512 devices in a mesh: chan: 16 (over y, core), rng: 32 (over x, z).
Axes of the slice: x: 4, y: 8, z: 8, core: 2. Of those that a mesh axis runs over, the one named last changes fastest.
Arguments:
- echoes: float32 [2, 512, 64, 4096], P(None, 'chan', None, 'rng'), may hold values from -6 to 6
- filter_taps: float32 [2, 512], replicated, may hold values from -0.1875 to 0.1875
Outputs:
- covariance: float32 [2, 64, 512, 512], P(None, 'rng', 'chan')
The draws below stay inside these ranges and needn't reach their ends.
All inputs are finite; a program needn't handle non-finite values.
Results may differ from the reference program's by a relative error of at most 0.0003.
Values sent between devices are 32-bit elements; how exact they have to be, the bound alone decides.
No kernel may reach another device: no remote copies, remote signals or barrier semaphores. Data moves between devices by JAX's collectives and lax.ppermute only.
A program may use at most 64 MiB of HBM per device.

```python
import math
import jax
import jax.numpy as jnp
from jax import lax

C = 512
P_SIZE = 64
TAPS = 512
GATES = 4096


def steps_of(key, dims, split, smallest, high):
    def one(position, blocks):
        draws = jax.random.uniform(jax.random.fold_in(jax.random.fold_in(key, 6), position), (blocks,), jnp.float32, smallest / len(split), high / len(split))
        return jnp.repeat(jnp.exp(draws), dims[position] // blocks).reshape((-1,) + (1,) * (len(dims) - position - 1))

    gain = one(*split[0])
    for cut in split[1:]:
        gain = gain * one(*cut)
    return gain


def gaussian(rng, extent, deviation, limit, split=(), kind=jnp.bfloat16):
    array = deviation * jax.random.normal(rng, extent, jnp.float32)
    if split:
        array = array * steps_of(rng, extent, split, -0.22, 0.18)
    return jnp.clip(array, -limit, limit).astype(kind)


def setup_inputs(seed: int = 0) -> dict:
    key_of = jax.random.split(jax.random.key(seed), 3)
    echoes = gaussian(key_of[0], (2, C, P_SIZE, GATES), 1.0, 6.0, ((1, 16), (3, 32)), jnp.float32)
    filter_taps = gaussian(key_of[1], (2, TAPS), (2 * TAPS) ** -0.5, 0.1875, (), jnp.float32)
    return dict(echoes=echoes, filter_taps=filter_taps)


def reference(echoes, filter_taps):
    pulse_count = echoes.shape[2]
    gate_count = echoes.shape[3]
    tap_count = filter_taps.shape[1]
    fft_len = gate_count + tap_count
    taps_cplx = filter_taps[0] + 1j * filter_taps[1]
    taps_spec = fft_len * jnp.fft.ifft(taps_cplx, n=fft_len)
    pulse_idx = jnp.arange(pulse_count, dtype=jnp.int32)
    norm_factor = 1.0 / math.sqrt(pulse_count)
    highest = lax.Precision.HIGHEST

    def one_bin(bin_index):
        phases = (bin_index * pulse_idx % pulse_count).astype(jnp.float32) * (2.0 * math.pi / pulse_count)
        cos_table = jnp.cos(phases)
        sin_table = jnp.sin(phases)
        spec_re = (jnp.einsum('cpg,p->cg', echoes[0], cos_table, precision=highest) + jnp.einsum('cpg,p->cg', echoes[1], sin_table, precision=highest)) * norm_factor
        spec_im = (jnp.einsum('cpg,p->cg', echoes[1], cos_table, precision=highest) - jnp.einsum('cpg,p->cg', echoes[0], sin_table, precision=highest)) * norm_factor
        filtered = jnp.fft.ifft(jnp.fft.fft(spec_re + 1j * spec_im, n=fft_len, axis=-1) * taps_spec, axis=-1)[:, :gate_count]
        out_re = jnp.real(filtered).astype(jnp.float32)
        out_im = jnp.imag(filtered).astype(jnp.float32)
        real_part = (jnp.dot(out_re, out_re.T, precision=highest, preferred_element_type=jnp.float32) + jnp.dot(out_im, out_im.T, precision=highest, preferred_element_type=jnp.float32)) / gate_count
        imag_part = (jnp.dot(out_im, out_re.T, precision=highest, preferred_element_type=jnp.float32) - jnp.dot(out_re, out_im.T, precision=highest, preferred_element_type=jnp.float32)) / gate_count
        return jnp.stack([real_part, imag_part])
    stacked = lax.map(one_bin, jnp.arange(pulse_count, dtype=jnp.int32))
    return jnp.transpose(stacked, (1, 0, 2, 3))
```

```python
import functools
import math

import jax
import jax.numpy as jnp
import ml_dtypes
import numpy as np
from jax import lax
from jax.experimental import pallas as pl
from jax.experimental.pallas import tpu as pltpu
from jax.sharding import Mesh
from jax.sharding import PartitionSpec as P

VMEM = pl.BlockSpec(memory_space=pltpu.VMEM)
SMEM = pl.BlockSpec(memory_space=pltpu.SMEM)
F32 = jnp.float32
BF16 = jnp.bfloat16
Y, CORE, X, Z = 8, 2, 4, 8


def halves(value):
    high = value.astype(BF16)
    return high, (value - high.astype(F32)).astype(BF16)


def dot3(left, right, dims):
    lh, ll = left
    rh, rl = right
    mul = lambda a, b: lax.dot_general(a, b, (dims, ((), ())), preferred_element_type=F32)
    return mul(lh, rh) + mul(ll, rh) + mul(lh, rl)


NN = ((1,), (0,))
NT = ((1,), (1,))


def params(mib):
    return pltpu.CompilerParams(vmem_limit_bytes=mib << 20)


def cost(flops, moved):
    return pl.CostEstimate(flops=int(flops), bytes_accessed=int(moved), transcendentals=0)


def doppler_table(pulses):
    order = np.arange(pulses)
    bins = (2 * Z) * (order % Y // 2) + 2 * (order // Y) + order % 2
    phase = (bins[:, None] * np.arange(pulses)[None, :] % pulses) * (2.0 * math.pi / pulses)
    cos, sin = np.cos(phase), np.sin(phase)
    re = np.concatenate([cos, sin], axis=1)
    im = np.concatenate([-sin, cos], axis=1)
    table = np.stack([re, im], axis=1).reshape(2 * pulses, 2 * pulses) / math.sqrt(pulses)
    table = table.astype(np.float32)
    high = table.astype(ml_dtypes.bfloat16)
    low = (table - high.astype(np.float32)).astype(ml_dtypes.bfloat16)
    return high, low


def doppler_kernel(x_ref, high_ref, low_ref, o_ref):
    channels = x_ref.shape[1]
    rows = high_ref.shape[0]
    table = (high_ref[...], low_ref[...])
    for c in range(0, channels, 2):
        pair = jnp.concatenate(
            [
                jnp.concatenate([x_ref[0, c], x_ref[0, c + 1]], axis=1),
                jnp.concatenate([x_ref[1, c], x_ref[1, c + 1]], axis=1),
            ],
            axis=0,
        )
        out = dot3(table, halves(pair), NN)
        lanes = out.shape[1] // 2
        o_ref[pl.ds(c, rows, stride=channels), :] = out[:, :lanes]
        o_ref[pl.ds(c + 1, rows, stride=channels), :] = out[:, lanes:]


def doppler(echoes):
    _, channels, pulses, gates = echoes.shape
    high, low = doppler_table(pulses)
    rows = 2 * pulses
    return pl.pallas_call(
        doppler_kernel,
        out_shape=jax.ShapeDtypeStruct((rows * channels, gates), F32),
        in_specs=[VMEM] * 3,
        out_specs=VMEM,
        compiler_params=params(24),
        cost_estimate=cost(6 * rows * rows * channels * gates, 16 * pulses * channels * gates),
        name="doppler",
    )(echoes, jnp.asarray(high), jnp.asarray(low))


def taps_kernel(taps_ref, high_ref, low_ref):
    steps = taps_ref.shape[1]
    width = taps_ref.shape[2]
    lag = lax.broadcasted_iota(jnp.int32, (width, width), 0) - lax.broadcasted_iota(jnp.int32, (width, width), 1)
    zero = jnp.zeros((1, width), F32)
    for k in range(steps + 1):
        block = []
        for part in range(2):
            later = taps_ref[part, k : k + 1, :] if k < steps else zero
            earlier = taps_ref[part, k - 1 : k, :] if k > 0 else zero
            line = jnp.concatenate([later, earlier], axis=1)
            turned = pltpu.roll(jnp.broadcast_to(line, (width, 2 * width)), 0, 1, stride=1, stride_axis=0)
            block.append(turned[:, :width].T)
        re, im = block
        table = jnp.concatenate(
            [jnp.concatenate([re, im], axis=1), jnp.concatenate([-im, re], axis=1)], axis=0
        )
        high, low = halves(table)
        high_ref[pl.ds(2 * width * k, 2 * width), :] = high
        low_ref[pl.ds(2 * width * k, 2 * width), :] = low


def tap_tables(filter_taps, width):
    parts, taps = filter_taps.shape
    steps = taps // width
    shape = jax.ShapeDtypeStruct((2 * width * (steps + 1), 2 * width), BF16)
    return pl.pallas_call(
        taps_kernel,
        out_shape=(shape, shape),
        in_specs=[VMEM],
        out_specs=(VMEM, VMEM),
        compiler_params=params(16),
        cost_estimate=cost(1e6, 2e6),
        name="tap_tables",
    )(filter_taps.reshape(parts, steps, width))


def load_blocks(ref, count, high_ref, low_ref):
    rows = ref.shape[0] // count
    half = ref.shape[1] // 2
    width = ref.shape[2]
    for n in range(count):
        for part in range(2):
            piece = ref[n * rows : (n + 1) * rows, part * half : (part + 1) * half, :]
            high, low = halves(piece.reshape(rows * half, width))
            lanes = slice((2 * n + part) * width, (2 * n + part + 1) * width)
            high_ref[:, lanes] = high
            low_ref[:, lanes] = low


def filter_kernel(x_ref, wh_ref, wl_ref, inner_ref, outer_ref, high, low):
    span = wh_ref.shape[1]
    blocks = Z
    load_blocks(x_ref, blocks, high, low)

    def term(first, last, lag):
        lanes = slice(first * span, last * span)
        rows = slice(lag * span, (lag + last - first) * span)
        return dot3((high[:, lanes], low[:, lanes]), (wh_ref[rows, :], wl_ref[rows, :]), NN)

    for j in range(4):
        inner_ref[j] = term(j, j + 5, 0)
    outer_ref[0] = term(0, 3, 2)
    outer_ref[1] = term(0, 4, 1)
    outer_ref[2] = term(4, 8, 0)
    outer_ref[3] = term(5, 8, 0)


def edge_kernel(first_ref, before_ref, after_ref, outer_ref, wh_ref, wl_ref, o_ref, bh, bl, ah, al):
    span = wh_ref.shape[1]
    load_blocks(before_ref, 2, bh, bl)
    load_blocks(after_ref, 2, ah, al)

    def term(high, low, first, last, lag):
        lanes = slice(first * span, last * span)
        rows = slice(lag * span, (lag + last - first) * span)
        return dot3((high[:, lanes], low[:, lanes]), (wh_ref[rows, :], wl_ref[rows, :]), NN)

    keep = first_ref[0] == 0
    zero = jnp.zeros(outer_ref.shape[1:], F32)
    o_ref[0] = jnp.where(keep, outer_ref[0], zero) + term(bh, bl, 0, 2, 0)
    o_ref[1] = jnp.where(keep, outer_ref[1], zero) + term(bh, bl, 1, 2, 0)
    o_ref[2] = outer_ref[2] + term(ah, al, 0, 1, 4)
    o_ref[3] = outer_ref[3] + term(ah, al, 0, 2, 3)


def gram_kernel(side_ref, own_ref, other_ref, *rest):
    before_ref = rest[0] if len(rest) == 6 else None
    o_ref, lh, ll, rh, rl = rest[-5:]
    blocks, rows, span = own_ref.shape
    width = span // 2
    group = rows // Y
    side = side_ref[0]
    for n in range(blocks):
        lanes = slice(n * span, (n + 1) * span)
        for source, place in ((own_ref, side), (other_ref, 1 - side)):
            high, low = halves(source[n])
            if source is own_ref:
                lh[:rows, lanes] = high
                ll[:rows, lanes] = low
                lh[rows:, lanes] = jnp.concatenate([high[:, width:], -high[:, :width]], axis=1)
                ll[rows:, lanes] = jnp.concatenate([low[:, width:], -low[:, :width]], axis=1)
            for y in range(Y):
                start = pl.multiple_of(y * 2 * group + place * group, group)
                rh[pl.ds(start, group), lanes] = high[y * group : (y + 1) * group]
                rl[pl.ds(start, group), lanes] = low[y * group : (y + 1) * group]
    right = (rh[...], rl[...])
    quarter = rows // X
    for part in range(2):
        here = slice(part * rows, (part + 1) * rows)
        out = dot3((lh[here, :], ll[here, :]), right, NT)
        for x in range(X):
            piece = out[x * quarter : (x + 1) * quarter]
            o_ref[x, part] = piece if before_ref is None else piece + before_ref[x, part]


def gram(side, own, other, before=None):
    blocks, rows, span = own.shape
    depth = blocks * span
    extra = [] if before is None else [before]
    return pl.pallas_call(
        gram_kernel,
        out_shape=jax.ShapeDtypeStruct((X, 2, rows // X, 2 * rows), F32),
        in_specs=[SMEM] + [VMEM] * (2 + len(extra)),
        out_specs=VMEM,
        scratch_shapes=[pltpu.VMEM((2 * rows, depth), BF16)] * 4,
        compiler_params=params(24),
        cost_estimate=cost(6 * 4 * rows * rows * depth, 8 * rows * depth),
        name="gram",
    )(side, own, other, *extra)


def per_device(echoes, filter_taps):
    width = echoes.shape[3]
    pulses = echoes.shape[2]
    gate_count = width * X * Z
    side = lax.axis_index("core").astype(jnp.int32).reshape(1)
    first = (lax.axis_index("x") == 0).astype(jnp.int32).reshape(1)
    odd = lax.axis_index("y") % 2 == 1

    sent = doppler(echoes)
    wh, wl = tap_tables(filter_taps, width)
    rows = 2 * echoes.shape[1]
    got = lax.all_to_all(sent.reshape(pulses, rows, width), ("z", "y"), 0, 0, tiled=True)
    before = lax.ppermute(got[(Z - 2) * Y :], "x", [(i, (i + 1) % X) for i in range(X)])
    after = lax.ppermute(got[: 2 * Y], "x", [(i, i - 1) for i in range(1, X)])

    channels = Y * rows // 2
    span = 2 * width
    block = jax.ShapeDtypeStruct((4, channels, span), F32)
    one = 6 * channels * span * span
    inner, outer = pl.pallas_call(
        filter_kernel,
        out_shape=(block, block),
        in_specs=[VMEM] * 3,
        out_specs=(VMEM, VMEM),
        scratch_shapes=[pltpu.VMEM((channels, Z * span), BF16)] * 2,
        compiler_params=params(24),
        cost_estimate=cost(34 * one, 6e6),
        name="filter_inner",
    )(got, wh, wl)
    swap = [(0, 1), (1, 0)]
    inner_other = lax.ppermute(inner, "core", swap)
    total = gram(side, inner, inner_other)
    edge = pl.pallas_call(
        edge_kernel,
        out_shape=block,
        in_specs=[SMEM] + [VMEM] * 5,
        out_specs=VMEM,
        scratch_shapes=[pltpu.VMEM((channels, 2 * span), BF16)] * 4,
        compiler_params=params(24),
        cost_estimate=cost(6 * one, 4e6),
        name="filter_edge",
    )(first, before, after, outer, wh, wl)
    edge_other = lax.ppermute(edge, "core", swap)
    total = gram(side, edge, edge_other, total)

    quarter = channels // X
    parts = lax.all_to_all(total.reshape(X, 2 * quarter, 2 * channels), "x", 0, 0, tiled=True)
    summed = jnp.sum(parts.reshape(X, 2, 2, quarter // 2, 2 * channels), axis=0) * (1.0 / gate_count)
    send = (
        jnp.where(odd, summed[:, 1], summed[:, 0]),
        jnp.where(odd, summed[:, 0], summed[:, 1]),
    )
    recv = []
    for turn in range(2):
        pairs = [
            (y * X + x, (2 * x + (turn ^ (y & 1))) * X + y // 2) for y in range(Y) for x in range(X)
        ]
        recv.append(lax.ppermute(send[turn], ("y", "x"), pairs))
    return jnp.stack(
        [jnp.where(odd, recv[1], recv[0]), jnp.where(odd, recv[0], recv[1])], axis=1
    )


def solution(mesh):
    split = Mesh(mesh.devices.reshape(Y, CORE, X, Z), ("y", "core", "x", "z"))
    in_specs = (P(None, ("y", "core"), None, ("x", "z")), P())
    out_specs = P(None, ("x", "z"), ("y", "core"), None)
    return jax.shard_map(
        per_device, mesh=split, in_specs=in_specs, out_specs=out_specs, check_vma=False
    )
```

```python
import functools
import math

import jax
import jax.numpy as jnp
import ml_dtypes
import numpy as np
from jax import lax
from jax.experimental import pallas as pl
from jax.experimental.pallas import tpu as pltpu
from jax.sharding import Mesh
from jax.sharding import PartitionSpec as P

VMEM = pl.BlockSpec(memory_space=pltpu.VMEM)
SMEM = pl.BlockSpec(memory_space=pltpu.SMEM)
F32 = jnp.float32
BF16 = jnp.bfloat16
Y, CORE, X, Z = 8, 2, 4, 8


def halves(value):
    high = value.astype(BF16)
    return high, (value - high.astype(F32)).astype(BF16)


def dot3(left, right, dims):
    lh, ll = left
    rh, rl = right
    mul = lambda a, b: lax.dot_general(a, b, (dims, ((), ())), preferred_element_type=F32)
    return mul(lh, rh) + mul(ll, rh) + mul(lh, rl)


NN = ((1,), (0,))
NT = ((1,), (1,))


def params(mib):
    return pltpu.CompilerParams(vmem_limit_bytes=mib << 20)


def cost(flops, moved):
    return pl.CostEstimate(flops=int(flops), bytes_accessed=int(moved), transcendentals=0)


def bin_of(z, y):
    return 2 * (Z * (y % X) + z) + y // X


def doppler_table(pulses):
    order = np.arange(pulses)
    bins = bin_of(order // Y, order % Y)
    phase = (bins[:, None] * np.arange(pulses)[None, :] % pulses) * (2.0 * math.pi / pulses)
    cos, sin = np.cos(phase), np.sin(phase)
    re = np.concatenate([cos, sin], axis=1)
    im = np.concatenate([-sin, cos], axis=1)
    table = np.stack([re, im], axis=1).reshape(2 * pulses, 2 * pulses) / math.sqrt(pulses)
    table = table.astype(np.float32)
    high = table.astype(ml_dtypes.bfloat16)
    low = (table - high.astype(np.float32)).astype(ml_dtypes.bfloat16)
    return np.stack([high, low])


def doppler_kernel(x_ref, table_ref, o_ref):
    channels = x_ref.shape[1]
    rows = table_ref.shape[1]
    table = (table_ref[0], table_ref[1])
    for c in range(0, channels, 2):
        pair = jnp.concatenate(
            [
                jnp.concatenate([x_ref[0, c], x_ref[0, c + 1]], axis=1),
                jnp.concatenate([x_ref[1, c], x_ref[1, c + 1]], axis=1),
            ],
            axis=0,
        )
        out = dot3(table, halves(pair), NN)
        lanes = out.shape[1] // 2
        o_ref[pl.ds(c, rows, stride=channels), :] = out[:, :lanes]
        o_ref[pl.ds(c + 1, rows, stride=channels), :] = out[:, lanes:]


def doppler(echoes):
    _, channels, pulses, gates = echoes.shape
    rows = 2 * pulses
    return pl.pallas_call(
        doppler_kernel,
        out_shape=jax.ShapeDtypeStruct((rows * channels, gates), F32),
        in_specs=[VMEM] * 2,
        out_specs=VMEM,
        compiler_params=params(12),
        cost_estimate=cost(6 * rows * rows * channels * gates, 16 * pulses * channels * gates),
        name="doppler",
    )(echoes, jnp.asarray(doppler_table(pulses)))


def tap_table(taps_ref, k):
    steps, width = taps_ref.shape[1:]
    zero = jnp.zeros((1, width), F32)
    block = []
    for part in range(2):
        later = taps_ref[part, k : k + 1, :] if k < steps else zero
        earlier = taps_ref[part, k - 1 : k, :] if k > 0 else zero
        line = jnp.concatenate([later, earlier], axis=1)
        turned = pltpu.roll(jnp.broadcast_to(line, (width, 2 * width)), 0, 1, stride=1, stride_axis=0)
        block.append(turned[:, :width].T)
    re, im = block
    return jnp.concatenate(
        [jnp.concatenate([re, im], axis=1), jnp.concatenate([-im, re], axis=1)], axis=0
    )


def fill_tables(taps_ref, wh_ref, wl_ref, lags):
    span = wh_ref.shape[1]
    for n, k in enumerate(lags):
        high, low = halves(tap_table(taps_ref, k))
        wh_ref[n * span : (n + 1) * span, :] = high
        wl_ref[n * span : (n + 1) * span, :] = low


def load_blocks(ref, count, high_ref, low_ref):
    rows = ref.shape[0] // count
    half = ref.shape[1] // 2
    width = ref.shape[2]
    for n in range(count):
        for part in range(2):
            piece = ref[n * rows : (n + 1) * rows, part * half : (part + 1) * half, :]
            high, low = halves(piece.reshape(rows * half, width))
            lanes = slice((2 * n + part) * width, (2 * n + part + 1) * width)
            high_ref[:, lanes] = high
            low_ref[:, lanes] = low


def filter_kernel(x_ref, taps_ref, inner_ref, outer_ref, high, low, wh_ref, wl_ref):
    span = wh_ref.shape[1]
    fill_tables(taps_ref, wh_ref, wl_ref, range(taps_ref.shape[1] + 1))
    blocks = Z
    load_blocks(x_ref, blocks, high, low)

    def term(first, last, lag):
        lanes = slice(first * span, last * span)
        rows = slice(lag * span, (lag + last - first) * span)
        return dot3((high[:, lanes], low[:, lanes]), (wh_ref[rows, :], wl_ref[rows, :]), NN)

    for j in range(4):
        inner_ref[j] = term(j, j + 5, 0)
    outer_ref[0] = term(0, 3, 2)
    outer_ref[1] = term(0, 4, 1)
    outer_ref[2] = term(4, 8, 0)
    outer_ref[3] = term(5, 8, 0)


def edge_kernel(first_ref, before_ref, after_ref, outer_ref, taps_ref, o_ref, bh, bl, ah, al, wh_ref, wl_ref):
    span = wh_ref.shape[1]
    lags = taps_ref.shape[1]
    fill_tables(taps_ref, wh_ref, wl_ref, (0, 1, lags - 1, lags))
    load_blocks(before_ref, 2, bh, bl)
    load_blocks(after_ref, 2, ah, al)

    def term(high, low, first, last, lag):
        lanes = slice(first * span, last * span)
        rows = slice(lag * span, (lag + last - first) * span)
        return dot3((high[:, lanes], low[:, lanes]), (wh_ref[rows, :], wl_ref[rows, :]), NN)

    keep = first_ref[0] == 0
    zero = jnp.zeros(outer_ref.shape[1:], F32)
    o_ref[0] = jnp.where(keep, outer_ref[0], zero) + term(bh, bl, 0, 2, 0)
    o_ref[1] = jnp.where(keep, outer_ref[1], zero) + term(bh, bl, 1, 2, 0)
    o_ref[2] = outer_ref[2] + term(ah, al, 0, 1, 3)
    o_ref[3] = outer_ref[3] + term(ah, al, 0, 2, 2)


def gram_kernel(place_ref, own_ref, other_ref, *rest):
    before_ref = rest[0] if len(rest) == 5 else None
    o_ref, left, right_high, right_low = rest[-4:]
    blocks, rows, span = own_ref.shape
    width = span // 2
    group = rows // Y
    side, at_y = place_ref[0], place_ref[1]
    for n in range(blocks):
        lanes = slice(n * span, (n + 1) * span)
        for source, turn in ((own_ref, side), (other_ref, 1 - side)):
            for part, right in zip(halves(source[n]), (right_high, right_low)):
                if source is own_ref:
                    top = 2 * rows if right is right_low else 0
                    left[top : top + rows, lanes] = part
                    left[top + rows : top + 2 * rows, lanes] = jnp.concatenate(
                        [part[:, width:], -part[:, :width]], axis=1
                    )
                for y in range(Y):
                    start = pl.multiple_of(y * 2 * group + turn * group, group)
                    right[pl.ds(start, group), lanes] = part[y * group : (y + 1) * group]
    mul = lambda a, b: lax.dot_general(a, b, (NT, ((), ())), preferred_element_type=F32)
    both = mul(left[...], right_high[...])
    out = both[: 2 * rows] + both[2 * rows :] + mul(left[: 2 * rows, :], right_low[...])
    for y in range(Y):
        x, turn = handed_to(y, at_y)
        for part in range(2):
            start = part * rows + y * group
            piece = out[start : start + group]
            if before_ref is not None:
                piece = piece + before_ref[x, turn, part]
            o_ref[x, turn, part] = piece


def handed_to(y, at_y):
    ahead = lax.rem(y - at_y + Y, Y)
    pair = lax.div(lax.rem(ahead + 1, Y), 2)
    x = lax.rem(at_y + 2 - pair + X, X)
    turn = lax.rem(ahead + 1 + lax.div(at_y, X), 2)
    return x, turn


def last_sends():
    sends = [[], []]
    for at_y in range(Y):
        for y in range(Y):
            ahead = (y - at_y) % Y
            x = (at_y + 2 - (ahead + 1) % Y // 2) % X
            turn = (ahead + 1 + at_y // X) % 2
            sends[turn].append((at_y * X + x, y * X + at_y % X))
    return sends


def gram(place, own, other, before=None):
    blocks, rows, span = own.shape
    depth = blocks * span
    extra = [] if before is None else [before]
    return pl.pallas_call(
        gram_kernel,
        out_shape=jax.ShapeDtypeStruct((X, 2, 2, rows // Y, 2 * rows), F32),
        in_specs=[SMEM] + [VMEM] * (2 + len(extra)),
        out_specs=VMEM,
        scratch_shapes=[pltpu.VMEM((4 * rows, depth), BF16)] + [pltpu.VMEM((2 * rows, depth), BF16)] * 2,
        compiler_params=params(16),
        cost_estimate=cost(6 * 4 * rows * rows * depth, 8 * rows * depth),
        name="gram",
    )(place, own, other, *extra)


def sum_kernel(scale, parts_ref, first_ref, second_ref):
    for turn, out in enumerate((first_ref, second_ref)):
        total = parts_ref[0, turn]
        for x in range(1, X):
            total = total + parts_ref[x, turn]
        out[...] = total * scale


def place_kernel(swap_ref, first_ref, second_ref, o_ref):
    swap = swap_ref[0]
    for part in range(2):
        o_ref[part, swap] = first_ref[part]
        o_ref[part, 1 - swap] = second_ref[part]


def per_device(echoes, filter_taps):
    width = echoes.shape[3]
    pulses = echoes.shape[2]
    gate_count = width * X * Z
    at_x, at_y = lax.axis_index("x"), lax.axis_index("y")
    place = jnp.stack([lax.axis_index("core"), at_y]).astype(jnp.int32)
    first = (at_x == 0).astype(jnp.int32).reshape(1)
    swapped = (at_y + at_x + 1 & 1).astype(jnp.int32).reshape(1)

    sent = doppler(echoes)
    taps = filter_taps.reshape(2, -1, width)
    rows = 2 * echoes.shape[1]
    got = lax.all_to_all(sent.reshape(pulses, rows, width), ("z", "y"), 0, 0, tiled=True)
    before = lax.ppermute(got[(Z - 2) * Y :], "x", [(i, (i + 1) % X) for i in range(X)])
    after = lax.ppermute(got[: 2 * Y], "x", [(i, i - 1) for i in range(1, X)])

    channels = Y * rows // 2
    span = 2 * width
    block = jax.ShapeDtypeStruct((4, channels, span), F32)
    one = 6 * channels * span * span
    inner, outer = pl.pallas_call(
        filter_kernel,
        out_shape=(block, block),
        in_specs=[VMEM] * 2,
        out_specs=(VMEM, VMEM),
        scratch_shapes=[pltpu.VMEM((channels, Z * span), BF16)] * 2
        + [pltpu.VMEM(((taps.shape[1] + 1) * span, span), BF16)] * 2,
        compiler_params=params(10),
        cost_estimate=cost(34 * one, 6e6),
        name="filter_inner",
    )(got, taps)
    swap = [(0, 1), (1, 0)]
    inner_other = lax.ppermute(inner, "core", swap)
    total = gram(place, inner, inner_other)
    edge = pl.pallas_call(
        edge_kernel,
        out_shape=block,
        in_specs=[SMEM] + [VMEM] * 4,
        out_specs=VMEM,
        scratch_shapes=[pltpu.VMEM((channels, 2 * span), BF16)] * 4
        + [pltpu.VMEM((4 * span, span), BF16)] * 2,
        compiler_params=params(10),
        cost_estimate=cost(6 * one, 4e6),
        name="filter_edge",
    )(first, before, after, outer, taps)
    edge_other = lax.ppermute(edge, "core", swap)
    total = gram(place, edge, edge_other, total)

    group = channels // Y
    parts = lax.all_to_all(total, "x", 0, 0, tiled=True)
    piece = jax.ShapeDtypeStruct((2, group, 2 * channels), F32)
    sends = pl.pallas_call(
        functools.partial(sum_kernel, 1.0 / gate_count),
        out_shape=(piece, piece),
        in_specs=[VMEM],
        out_specs=(VMEM, VMEM),
        compiler_params=params(4),
        cost_estimate=cost(1e6, 2e6),
        name="add_up",
    )(parts)
    got = [lax.ppermute(part, ("y", "x"), pairs) for part, pairs in zip(sends, last_sends())]
    return pl.pallas_call(
        place_kernel,
        out_shape=jax.ShapeDtypeStruct((2, 2, group, 2 * channels), F32),
        in_specs=[SMEM, VMEM, VMEM],
        out_specs=VMEM,
        compiler_params=params(4),
        cost_estimate=cost(1e5, 1e6),
        name="place",
    )(swapped, *got)


def solution(mesh):
    split = Mesh(mesh.devices.reshape(Y, CORE, X, Z), ("y", "core", "x", "z"))
    in_specs = (P(None, ("y", "core"), None, ("x", "z")), P())
    out_specs = P(None, ("x", "z"), ("y", "core"), None)
    return jax.shard_map(
        per_device, mesh=split, in_specs=in_specs, out_specs=out_specs, check_vma=False
    )
```

```python
import functools
import math

import jax
import jax.numpy as jnp
from jax import lax
from jax.experimental import pallas as pl
from jax.experimental.pallas import tpu as pltpu
from jax.sharding import Mesh
from jax.sharding import PartitionSpec as P

VMEM = pl.BlockSpec(memory_space=pltpu.VMEM)
SMEM = pl.BlockSpec(memory_space=pltpu.SMEM)
F32 = jnp.float32
BF16 = jnp.bfloat16
Y, CORE, X, Z = 8, 2, 4, 8


def halves(value):
    high = value.astype(BF16)
    return high, (value - high.astype(F32)).astype(BF16)


def dot3(left, right, dims):
    lh, ll = left
    rh, rl = right
    mul = lambda a, b: lax.dot_general(a, b, (dims, ((), ())), preferred_element_type=F32)
    return mul(lh, rh) + mul(ll, rh) + mul(lh, rl)


NN = ((1,), (0,))
NT = ((1,), (1,))


def params(mib):
    return pltpu.CompilerParams(vmem_limit_bytes=mib << 20)


def cost(flops, moved):
    return pl.CostEstimate(flops=int(flops), bytes_accessed=int(moved), transcendentals=0)


def bin_of(z, y):
    return 2 * (Z * (y % X) + z) + y // X


def doppler_table(pulses):
    shape = (2 * pulses, 2 * pulses)
    row = lax.broadcasted_iota(jnp.int32, shape, 0)
    column = lax.broadcasted_iota(jnp.int32, shape, 1)
    target = lax.shift_right_logical(row, 1)
    y, z = target & (Y - 1), lax.shift_right_logical(target, Y.bit_length() - 1)
    bins = 2 * (Z * (y & (X - 1)) + z) + lax.shift_right_logical(y, X.bit_length() - 1)
    pulse = column & (pulses - 1)
    part = lax.shift_right_logical(column, pulses.bit_length() - 1)
    steps = bins * pulse + ((row & 1) - part) * (pulses // 4) & (pulses - 1)
    table = jnp.cos(steps.astype(F32) * (2.0 * math.pi / pulses)) * (1.0 / math.sqrt(pulses))
    return halves(table)


def doppler_kernel(x_ref, o_ref):
    _, channels, pulses, lanes = x_ref.shape
    rows = 2 * pulses
    table = doppler_table(pulses)
    for c in range(0, channels, 2):
        pair = jnp.concatenate(
            [
                jnp.concatenate([x_ref[0, c], x_ref[0, c + 1]], axis=1),
                jnp.concatenate([x_ref[1, c], x_ref[1, c + 1]], axis=1),
            ],
            axis=0,
        )
        out = dot3(table, halves(pair), NN)
        o_ref[pl.ds(c, rows, stride=channels), :] = out[:, :lanes]
        o_ref[pl.ds(c + 1, rows, stride=channels), :] = out[:, lanes:]


def doppler(echoes):
    _, channels, pulses, gates = echoes.shape
    rows = 2 * pulses
    return pl.pallas_call(
        doppler_kernel,
        out_shape=jax.ShapeDtypeStruct((rows * channels, gates), F32),
        in_specs=[VMEM],
        out_specs=VMEM,
        compiler_params=params(12),
        cost_estimate=cost(6 * rows * rows * channels * gates, 16 * pulses * channels * gates),
        name="doppler",
    )(echoes)


def tap_table(taps_ref, k):
    steps, width = taps_ref.shape[1:]
    zero = jnp.zeros((1, width), F32)
    block = []
    for part in range(2):
        later = taps_ref[part, k : k + 1, :] if k < steps else zero
        earlier = taps_ref[part, k - 1 : k, :] if k > 0 else zero
        line = jnp.concatenate([later, earlier], axis=1)
        turned = pltpu.roll(jnp.broadcast_to(line, (width, 2 * width)), 0, 1, stride=1, stride_axis=0)
        block.append(turned[:, :width].T)
    re, im = block
    return jnp.concatenate(
        [jnp.concatenate([re, im], axis=1), jnp.concatenate([-im, re], axis=1)], axis=0
    )


def fill_tables(taps_ref, wh_ref, wl_ref, lags):
    span = wh_ref.shape[1]
    for n, k in enumerate(lags):
        high, low = halves(tap_table(taps_ref, k))
        wh_ref[n * span : (n + 1) * span, :] = high
        wl_ref[n * span : (n + 1) * span, :] = low


def load_blocks(ref, count, high_ref, low_ref):
    rows = ref.shape[0] // count
    half = ref.shape[1] // 2
    width = ref.shape[2]
    for n in range(count):
        for part in range(2):
            piece = ref[n * rows : (n + 1) * rows, part * half : (part + 1) * half, :]
            high, low = halves(piece.reshape(rows * half, width))
            lanes = slice((2 * n + part) * width, (2 * n + part + 1) * width)
            high_ref[:, lanes] = high
            low_ref[:, lanes] = low


def filter_kernel(x_ref, taps_ref, inner_ref, outer_ref, high, low, wh_ref, wl_ref):
    span = wh_ref.shape[1]
    fill_tables(taps_ref, wh_ref, wl_ref, range(taps_ref.shape[1] + 1))
    blocks = Z
    load_blocks(x_ref, blocks, high, low)

    def term(first, last, lag):
        lanes = slice(first * span, last * span)
        rows = slice(lag * span, (lag + last - first) * span)
        return dot3((high[:, lanes], low[:, lanes]), (wh_ref[rows, :], wl_ref[rows, :]), NN)

    for j in range(4):
        inner_ref[j] = term(j, j + 5, 0)
    outer_ref[0] = term(0, 3, 2)
    outer_ref[1] = term(0, 4, 1)
    outer_ref[2] = term(4, 8, 0)
    outer_ref[3] = term(5, 8, 0)


def edge_kernel(
    first_ref, before_hbm, after_hbm, outer_ref, taps_ref, o_ref, bh, bl, ah, al, wh_ref, wl_ref, borders, sems
):
    span = wh_ref.shape[1]
    lags = taps_ref.shape[1]
    copies = [
        pltpu.make_async_copy(source, borders.at[n], sems.at[n]) for n, source in enumerate((before_hbm, after_hbm))
    ]
    for copy in copies:
        copy.start()
    fill_tables(taps_ref, wh_ref, wl_ref, (0, 1, lags - 1, lags))
    copies[0].wait()
    load_blocks(borders.at[0], 2, bh, bl)
    copies[1].wait()
    load_blocks(borders.at[1], 2, ah, al)

    def term(high, low, first, last, lag):
        lanes = slice(first * span, last * span)
        rows = slice(lag * span, (lag + last - first) * span)
        return dot3((high[:, lanes], low[:, lanes]), (wh_ref[rows, :], wl_ref[rows, :]), NN)

    keep = first_ref[0] == 0
    zero = jnp.zeros(outer_ref.shape[1:], F32)
    o_ref[0] = jnp.where(keep, outer_ref[0], zero) + term(bh, bl, 0, 2, 0)
    o_ref[1] = jnp.where(keep, outer_ref[1], zero) + term(bh, bl, 1, 2, 0)
    o_ref[2] = outer_ref[2] + term(ah, al, 0, 1, 3)
    o_ref[3] = outer_ref[3] + term(ah, al, 0, 2, 2)


def left_factor(own_ref, ref):
    blocks, rows, span = own_ref.shape
    width = span // 2
    for n in range(blocks):
        lanes = slice(n * span, (n + 1) * span)
        for top, part in zip((0, 2 * rows), halves(own_ref[n])):
            ref[top : top + rows, lanes] = part
            ref[top + rows : top + 2 * rows, lanes] = jnp.concatenate(
                [part[:, width:], -part[:, :width]], axis=1
            )


def right_factor(other_ref, ref):
    blocks, rows, span = other_ref.shape
    for n in range(blocks):
        for top, part in zip((0, rows), halves(other_ref[n])):
            ref[top : top + rows, n * span : (n + 1) * span] = part


def product(left, right):
    rows = left.shape[0] // 4
    mul = lambda a, b: lax.dot_general(a, b, (NT, ((), ())), preferred_element_type=F32)
    high = left[:rows, :] if right is None else right[:rows, :]
    low = left[2 * rows : 3 * rows, :] if right is None else right[rows:, :]
    both = mul(left[...], high)
    return both[: 2 * rows] + both[2 * rows :] + mul(left[: 2 * rows, :], low)


def own_kernel(own_ref, o_ref, left):
    left_factor(own_ref, left)
    o_ref[...] = product(left, None)


def middle_kernel(own_ref, other_ref, edge_ref, here_ref, there_ref, left, right):
    left_factor(own_ref, left)
    right_factor(other_ref, right)
    there_ref[...] = product(left, right)
    left_factor(edge_ref, left)
    here_ref[...] = product(left, None)


def last_kernel(place_ref, own_ref, other_ref, before_ref, here_ref, there_ref, o_ref, left, right):
    left_factor(own_ref, left)
    right_factor(other_ref, right)
    there = there_ref[...] + product(left, right)
    rows = here_ref.shape[1]
    group = rows // Y
    for y in range(Y):
        x, turn = handed_to(y, place_ref[0])
        for part in range(2):
            start = part * rows + y * group
            here = slice(start, start + group)
            o_ref[x, turn, part, :, :rows] = before_ref[here, :] + here_ref[here, :]
            o_ref[x, turn, part, :, rows:] = there[start : start + group]


def handed_to(y, at_y):
    ahead = lax.rem(y - at_y + Y, Y)
    pair = lax.div(lax.rem(ahead + 1, Y), 2)
    x = lax.rem(at_y + 2 - pair + X, X)
    turn = lax.rem(ahead + 1 + lax.div(at_y, X), 2)
    return x, turn


def last_sends():
    sends = [[], []]
    for at_y in range(Y):
        for y in range(Y):
            ahead = (y - at_y) % Y
            x = (at_y + 2 - (ahead + 1) % Y // 2) % X
            turn = (ahead + 1 + at_y // X) % 2
            sends[turn].append((at_y * X + x, y * X + at_y % X))
    return sends


def call(kernel, out_shape, scratch, flops, moved, name, *operands, place=None):
    scalars = [] if place is None else [place]
    return pl.pallas_call(
        kernel,
        out_shape=out_shape,
        in_specs=[SMEM] * len(scalars) + [VMEM] * len(operands),
        out_specs=jax.tree.map(lambda _: VMEM, out_shape),
        scratch_shapes=scratch,
        compiler_params=params(12),
        cost_estimate=cost(flops, moved),
        name=name,
    )(*scalars, *operands)


def sum_kernel(scale, parts_ref, first_ref, second_ref):
    for turn, out in enumerate((first_ref, second_ref)):
        total = parts_ref[0, turn]
        for x in range(1, X):
            total = total + parts_ref[x, turn]
        out[...] = total * scale


def place_kernel(swap_ref, first_ref, second_ref, o_ref):
    swap, side = swap_ref[0], swap_ref[1]
    rows = o_ref.shape[3] // 2
    group = rows // Y
    tile = 4 * group
    lane = lax.broadcasted_iota(jnp.int32, (o_ref.shape[2], tile), 1)
    odd, late = (lane & group) != 0, lane >= 2 * group
    for source, place in ((first_ref, swap), (second_ref, 1 - swap)):
        for part in range(2):
            own, other = source[part, :, :rows], source[part, :, rows:]
            low, high = jnp.where(side == 0, own, other), jnp.where(side == 0, other, own)
            for y in range(0, Y, 2):
                here = slice(y * group // tile * tile, y * group // tile * tile + tile)
                ahead = y * group % tile
                turned = [
                    pltpu.roll(values[:, here], (n * group - ahead - n // 2 * group) % tile, 1)
                    for n, values in enumerate((low, high, low, high))
                ]
                pair = [jnp.where(odd, turned[n + 1], turned[n]) for n in (0, 2)]
                o_ref[part, place, :, 2 * y * group : 2 * y * group + tile] = jnp.where(late, pair[1], pair[0])


def border_kernel(x_ref, low_ref, high_ref, sems):
    count = low_ref.shape[0]
    copies = [
        pltpu.make_async_copy(x_ref.at[pl.ds(start, count)], out, sems.at[n])
        for n, (start, out) in enumerate(((0, low_ref), (x_ref.shape[0] - count, high_ref)))
    ]
    for copy in copies:
        copy.start()
    for copy in copies:
        copy.wait()


def per_device(echoes, filter_taps):
    width = echoes.shape[3]
    pulses = echoes.shape[2]
    gate_count = width * X * Z
    at_x, at_y = lax.axis_index("x"), lax.axis_index("y")
    first = (at_x == 0).astype(jnp.int32).reshape(1)
    swapped = jnp.stack([at_y + at_x + 1 & 1, lax.axis_index("core")]).astype(jnp.int32)

    sent = doppler(echoes)
    taps = filter_taps.reshape(2, -1, width)
    rows = 2 * echoes.shape[1]
    got = lax.all_to_all(sent.reshape(pulses, rows, width), ("z", "y"), 0, 0, tiled=True)
    border = jax.ShapeDtypeStruct((2 * Y, rows, width), F32)
    low, high = pl.pallas_call(
        border_kernel,
        out_shape=(border, border),
        in_specs=[VMEM],
        out_specs=(pl.BlockSpec(memory_space=pltpu.HBM),) * 2,
        scratch_shapes=[pltpu.SemaphoreType.DMA((2,))],
        compiler_params=params(2),
        cost_estimate=cost(1e4, 2e6),
        name="borders",
    )(got)
    before = lax.ppermute(high, "x", [(i, (i + 1) % X) for i in range(X)])
    after = lax.ppermute(low, "x", [(i, i - 1) for i in range(1, X)])

    channels = Y * rows // 2
    span = 2 * width
    block = jax.ShapeDtypeStruct((4, channels, span), F32)
    one = 6 * channels * span * span
    inner, outer = pl.pallas_call(
        filter_kernel,
        out_shape=(block, block),
        in_specs=[VMEM] * 2,
        out_specs=(VMEM, VMEM),
        scratch_shapes=[pltpu.VMEM((channels, Z * span), BF16)] * 2
        + [pltpu.VMEM(((taps.shape[1] + 1) * span, span), BF16)] * 2,
        compiler_params=params(10),
        cost_estimate=cost(34 * one, 6e6),
        name="filter_inner",
    )(got, taps)
    swap = [(0, 1), (1, 0)]
    inner_other = lax.ppermute(inner, "core", swap)
    depth = 4 * span
    left = pltpu.VMEM((4 * channels, depth), BF16)
    right = pltpu.VMEM((2 * channels, depth), BF16)
    square = jax.ShapeDtypeStruct((2 * channels, channels), F32)
    unit = 6 * 2 * channels * channels * depth
    here = call(own_kernel, square, [left], unit, 3e6, "own_inner", inner)
    outer, here = lax.optimization_barrier((outer, here))
    edge = pl.pallas_call(
        edge_kernel,
        out_shape=block,
        in_specs=[SMEM] + [pl.BlockSpec(memory_space=pltpu.HBM)] * 2 + [VMEM] * 2,
        out_specs=VMEM,
        scratch_shapes=[pltpu.VMEM((channels, 2 * span), BF16)] * 4
        + [pltpu.VMEM((4 * span, span), BF16)] * 2
        + [pltpu.VMEM((2,) + border.shape, F32), pltpu.SemaphoreType.DMA((2,))],
        compiler_params=params(10),
        cost_estimate=cost(6 * one, 4e6),
        name="filter_edge",
    )(first, before, after, outer, taps)
    edge_other = lax.ppermute(edge, "core", swap)
    here_edge, there = call(
        middle_kernel, (square, square), [left, right], 2 * unit, 6e6, "other_inner", inner, inner_other, edge
    )
    group = channels // Y
    spread = jax.ShapeDtypeStruct((X, 2, 2, group, 2 * channels), F32)
    total = call(
        last_kernel, spread, [left, right], unit, 5e6, "other_edge", edge, edge_other, here, here_edge, there,
        place=at_y.astype(jnp.int32).reshape(1),
    )

    parts = lax.all_to_all(total, "x", 0, 0, tiled=True)
    piece = jax.ShapeDtypeStruct((2, group, 2 * channels), F32)
    sends = pl.pallas_call(
        functools.partial(sum_kernel, 1.0 / gate_count),
        out_shape=(piece, piece),
        in_specs=[VMEM],
        out_specs=(VMEM, VMEM),
        compiler_params=params(4),
        cost_estimate=cost(1e6, 2e6),
        name="add_up",
    )(parts)
    got = [lax.ppermute(part, ("y", "x"), pairs) for part, pairs in zip(sends, last_sends())]
    return pl.pallas_call(
        place_kernel,
        out_shape=jax.ShapeDtypeStruct((2, 2, group, 2 * channels), F32),
        in_specs=[SMEM, VMEM, VMEM],
        out_specs=VMEM,
        compiler_params=params(4),
        cost_estimate=cost(1e5, 1e6),
        name="place",
    )(swapped, *got)


def solution(mesh):
    split = Mesh(mesh.devices.reshape(Y, CORE, X, Z), ("y", "core", "x", "z"))
    in_specs = (P(None, ("y", "core"), None, ("x", "z")), P())
    out_specs = P(None, ("x", "z"), ("y", "core"), None)
    return jax.shard_map(
        per_device, mesh=split, in_specs=in_specs, out_specs=out_specs, check_vma=False
    )
```

```python
import functools
import math

import jax
import jax.numpy as jnp
from jax import lax
from jax.experimental import pallas as pl
from jax.experimental.pallas import tpu as pltpu
from jax.sharding import Mesh
from jax.sharding import PartitionSpec as P

VMEM = pl.BlockSpec(memory_space=pltpu.VMEM)
SMEM = pl.BlockSpec(memory_space=pltpu.SMEM)
F32 = jnp.float32
BF16 = jnp.bfloat16
Y, CORE, X, Z = 8, 2, 4, 8


def halves(value):
    high = value.astype(BF16)
    return high, (value - high.astype(F32)).astype(BF16)


def dot3(left, right, dims):
    lh, ll = left
    rh, rl = right
    mul = lambda a, b: lax.dot_general(a, b, (dims, ((), ())), preferred_element_type=F32)
    return mul(lh, rh) + mul(ll, rh) + mul(lh, rl)


NN = ((1,), (0,))
NT = ((1,), (1,))


def params(mib):
    return pltpu.CompilerParams(vmem_limit_bytes=mib << 20)


def cost(flops, moved):
    return pl.CostEstimate(flops=int(flops), bytes_accessed=int(moved), transcendentals=0)


def bin_of(z, y):
    return 2 * (Z * (y % X) + z) + y // X


def doppler_table(pulses):
    shape = (2 * pulses, 2 * pulses)
    row = lax.broadcasted_iota(jnp.int32, shape, 0)
    column = lax.broadcasted_iota(jnp.int32, shape, 1)
    target = lax.shift_right_logical(row, 1)
    y, z = target & (Y - 1), lax.shift_right_logical(target, Y.bit_length() - 1)
    bins = 2 * (Z * (y & (X - 1)) + z) + lax.shift_right_logical(y, X.bit_length() - 1)
    pulse = column & (pulses - 1)
    part = lax.shift_right_logical(column, pulses.bit_length() - 1)
    steps = bins * pulse + ((row & 1) - part) * (pulses // 4) & (pulses - 1)
    table = jnp.cos(steps.astype(F32) * (2.0 * math.pi / pulses)) * (1.0 / math.sqrt(pulses))
    return halves(table)


GROUPS = 4


def doppler_kernel(x_hbm, o_ref, x_ref, sems):
    _, channels, pulses, lanes = x_ref.shape
    rows = 2 * pulses
    group = channels // GROUPS
    copies = []
    for n in range(GROUPS):
        here = pl.ds(n * group, group)
        copies.append(pltpu.make_async_copy(x_hbm.at[:, here], x_ref.at[:, here], sems.at[n]))
        copies[-1].start()
    table = doppler_table(pulses)
    for c in range(0, channels, 2):
        if c % group == 0:
            copies[c // group].wait()
        pair = jnp.concatenate(
            [
                jnp.concatenate([x_ref[0, c], x_ref[0, c + 1]], axis=1),
                jnp.concatenate([x_ref[1, c], x_ref[1, c + 1]], axis=1),
            ],
            axis=0,
        )
        out = dot3(table, halves(pair), NN)
        o_ref[pl.ds(c, rows, stride=channels), :] = out[:, :lanes]
        o_ref[pl.ds(c + 1, rows, stride=channels), :] = out[:, lanes:]


def doppler(echoes):
    _, channels, pulses, gates = echoes.shape
    rows = 2 * pulses
    return pl.pallas_call(
        doppler_kernel,
        out_shape=jax.ShapeDtypeStruct((rows * channels, gates), F32),
        in_specs=[pl.BlockSpec(memory_space=pltpu.HBM)],
        out_specs=VMEM,
        scratch_shapes=[pltpu.VMEM(echoes.shape, F32), pltpu.SemaphoreType.DMA((GROUPS,))],
        compiler_params=params(51),
        cost_estimate=cost(6 * rows * rows * channels * gates, 16 * pulses * channels * gates),
        name="doppler",
    )(echoes)


def tap_table(taps_ref, k):
    steps, width = taps_ref.shape[1:]
    zero = jnp.zeros((1, width), F32)
    block = []
    for part in range(2):
        later = taps_ref[part, k : k + 1, :] if k < steps else zero
        earlier = taps_ref[part, k - 1 : k, :] if k > 0 else zero
        line = jnp.concatenate([later, earlier], axis=1)
        turned = pltpu.roll(jnp.broadcast_to(line, (width, 2 * width)), 0, 1, stride=1, stride_axis=0)
        block.append(turned[:, :width].T)
    re, im = block
    return jnp.concatenate(
        [jnp.concatenate([re, im], axis=1), jnp.concatenate([-im, re], axis=1)], axis=0
    )


def fill_tables(taps_ref, wh_ref, wl_ref, lags):
    span = wh_ref.shape[1]
    for n, k in enumerate(lags):
        high, low = halves(tap_table(taps_ref, k))
        wh_ref[n * span : (n + 1) * span, :] = high
        wl_ref[n * span : (n + 1) * span, :] = low


def load_blocks(ref, count, high_ref, low_ref):
    rows = ref.shape[0] // count
    half = ref.shape[1] // 2
    width = ref.shape[2]
    for n in range(count):
        for part in range(2):
            piece = ref[n * rows : (n + 1) * rows, part * half : (part + 1) * half, :]
            high, low = halves(piece.reshape(rows * half, width))
            lanes = slice((2 * n + part) * width, (2 * n + part + 1) * width)
            high_ref[:, lanes] = high
            low_ref[:, lanes] = low


def filter_kernel(x_ref, taps_ref, inner_ref, outer_ref, high, low, wh_ref, wl_ref):
    span = wh_ref.shape[1]
    fill_tables(taps_ref, wh_ref, wl_ref, range(taps_ref.shape[1] + 1))
    blocks = Z
    load_blocks(x_ref, blocks, high, low)

    def term(first, last, lag):
        lanes = slice(first * span, last * span)
        rows = slice(lag * span, (lag + last - first) * span)
        return dot3((high[:, lanes], low[:, lanes]), (wh_ref[rows, :], wl_ref[rows, :]), NN)

    for j in range(4):
        inner_ref[j] = term(j, j + 5, 0)
    outer_ref[0] = term(0, 3, 2)
    outer_ref[1] = term(0, 4, 1)
    outer_ref[2] = term(4, 8, 0)
    outer_ref[3] = term(5, 8, 0)


def edge_kernel(
    first_ref, before_hbm, after_hbm, outer_ref, taps_ref, o_ref, bh, bl, ah, al, wh_ref, wl_ref, borders, sems
):
    span = wh_ref.shape[1]
    lags = taps_ref.shape[1]
    copies = [
        pltpu.make_async_copy(source, borders.at[n], sems.at[n]) for n, source in enumerate((before_hbm, after_hbm))
    ]
    for copy in copies:
        copy.start()
    fill_tables(taps_ref, wh_ref, wl_ref, (0, 1, lags - 1, lags))
    copies[0].wait()
    load_blocks(borders.at[0], 2, bh, bl)

    def term(high, low, first, last, lag):
        lanes = slice(first * span, last * span)
        rows = slice(lag * span, (lag + last - first) * span)
        return dot3((high[:, lanes], low[:, lanes]), (wh_ref[rows, :], wl_ref[rows, :]), NN)

    keep = first_ref[0] == 0
    zero = jnp.zeros(outer_ref.shape[1:], F32)
    o_ref[0] = jnp.where(keep, outer_ref[0], zero) + term(bh, bl, 0, 2, 0)
    o_ref[1] = jnp.where(keep, outer_ref[1], zero) + term(bh, bl, 1, 2, 0)
    copies[1].wait()
    load_blocks(borders.at[1], 2, ah, al)
    o_ref[2] = outer_ref[2] + term(ah, al, 0, 1, 3)
    o_ref[3] = outer_ref[3] + term(ah, al, 0, 2, 2)


def left_factor(own_ref, ref):
    blocks, rows, span = own_ref.shape
    width = span // 2
    for n in range(blocks):
        lanes = slice(n * span, (n + 1) * span)
        for top, part in zip((0, 2 * rows), halves(own_ref[n])):
            ref[top : top + rows, lanes] = part
            ref[top + rows : top + 2 * rows, lanes] = jnp.concatenate(
                [part[:, width:], -part[:, :width]], axis=1
            )


def right_factor(other_ref, ref):
    blocks, rows, span = other_ref.shape
    for n in range(blocks):
        for top, part in zip((0, rows), halves(other_ref[n])):
            ref[top : top + rows, n * span : (n + 1) * span] = part


def product(left, right):
    rows = left.shape[0] // 4
    mul = lambda a, b: lax.dot_general(a, b, (NT, ((), ())), preferred_element_type=F32)
    high = left[:rows, :] if right is None else right[:rows, :]
    low = left[2 * rows : 3 * rows, :] if right is None else right[rows:, :]
    both = mul(left[...], high)
    return both[: 2 * rows] + both[2 * rows :] + mul(left[: 2 * rows, :], low)


def own_kernel(own_ref, o_ref, left):
    left_factor(own_ref, left)
    o_ref[...] = product(left, None)


def middle_kernel(own_ref, other_ref, edge_ref, here_ref, there_ref, left, right):
    left_factor(own_ref, left)
    right_factor(other_ref, right)
    there_ref[...] = product(left, right)
    left_factor(edge_ref, left)
    here_ref[...] = product(left, None)


def last_kernel(place_ref, own_ref, other_ref, before_ref, here_ref, there_ref, o_ref, left, right):
    left_factor(own_ref, left)
    right_factor(other_ref, right)
    there = there_ref[...] + product(left, right)
    rows = here_ref.shape[1]
    group = rows // Y
    for y in range(Y):
        x, turn = handed_to(y, place_ref[0])
        for part in range(2):
            start = part * rows + y * group
            here = slice(start, start + group)
            o_ref[x, turn, part, :, :rows] = before_ref[here, :] + here_ref[here, :]
            o_ref[x, turn, part, :, rows:] = there[start : start + group]


def handed_to(y, at_y):
    ahead = lax.rem(y - at_y + Y, Y)
    pair = lax.div(lax.rem(ahead + 1, Y), 2)
    x = lax.rem(at_y + 2 - pair + X, X)
    turn = lax.rem(ahead + 1 + lax.div(at_y, X), 2)
    return x, turn


def last_sends():
    sends = [[], []]
    for at_y in range(Y):
        for y in range(Y):
            ahead = (y - at_y) % Y
            x = (at_y + 2 - (ahead + 1) % Y // 2) % X
            turn = (ahead + 1 + at_y // X) % 2
            sends[turn].append((at_y * X + x, y * X + at_y % X))
    return sends


def call(kernel, out_shape, scratch, flops, moved, name, *operands, place=None):
    scalars = [] if place is None else [place]
    return pl.pallas_call(
        kernel,
        out_shape=out_shape,
        in_specs=[SMEM] * len(scalars) + [VMEM] * len(operands),
        out_specs=jax.tree.map(lambda _: VMEM, out_shape),
        scratch_shapes=scratch,
        compiler_params=params(12),
        cost_estimate=cost(flops, moved),
        name=name,
    )(*scalars, *operands)


def sum_kernel(scale, parts_ref, first_ref, second_ref):
    for turn, out in enumerate((first_ref, second_ref)):
        total = parts_ref[0, turn]
        for x in range(1, X):
            total = total + parts_ref[x, turn]
        out[...] = total * scale


def place_kernel(swap_ref, first_ref, second_ref, o_ref):
    swap, side = swap_ref[0], swap_ref[1]
    rows = o_ref.shape[3] // 2
    group = rows // Y
    tile = 4 * group
    lane = lax.broadcasted_iota(jnp.int32, (o_ref.shape[2], tile), 1)
    odd, late = (lane & group) != 0, lane >= 2 * group
    for source, place in ((first_ref, swap), (second_ref, 1 - swap)):
        for part in range(2):
            own, other = source[part, :, :rows], source[part, :, rows:]
            low, high = jnp.where(side == 0, own, other), jnp.where(side == 0, other, own)
            for y in range(0, Y, 2):
                here = slice(y * group // tile * tile, y * group // tile * tile + tile)
                ahead = y * group % tile
                turned = [
                    pltpu.roll(values[:, here], (n * group - ahead - n // 2 * group) % tile, 1)
                    for n, values in enumerate((low, high, low, high))
                ]
                pair = [jnp.where(odd, turned[n + 1], turned[n]) for n in (0, 2)]
                o_ref[part, place, :, 2 * y * group : 2 * y * group + tile] = jnp.where(late, pair[1], pair[0])


def border_kernel(x_ref, low_ref, high_ref, sems):
    count = low_ref.shape[0]
    copies = [
        pltpu.make_async_copy(x_ref.at[pl.ds(start, count)], out, sems.at[n])
        for n, (start, out) in enumerate(((0, low_ref), (x_ref.shape[0] - count, high_ref)))
    ]
    for copy in copies:
        copy.start()
    for copy in copies:
        copy.wait()


def per_device(echoes, filter_taps):
    width = echoes.shape[3]
    pulses = echoes.shape[2]
    gate_count = width * X * Z
    at_x, at_y = lax.axis_index("x"), lax.axis_index("y")
    first = (at_x == 0).astype(jnp.int32).reshape(1)
    swapped = jnp.stack([at_y + at_x + 1 & 1, lax.axis_index("core")]).astype(jnp.int32)

    sent = doppler(echoes)
    taps = filter_taps.reshape(2, -1, width)
    rows = 2 * echoes.shape[1]
    got = lax.all_to_all(sent.reshape(pulses, rows, width), ("z", "y"), 0, 0, tiled=True)
    border = jax.ShapeDtypeStruct((2 * Y, rows, width), F32)
    low, high = pl.pallas_call(
        border_kernel,
        out_shape=(border, border),
        in_specs=[VMEM],
        out_specs=(pl.BlockSpec(memory_space=pltpu.HBM),) * 2,
        scratch_shapes=[pltpu.SemaphoreType.DMA((2,))],
        compiler_params=params(2),
        cost_estimate=cost(1e4, 2e6),
        name="borders",
    )(got)
    before = lax.ppermute(high, "x", [(i, (i + 1) % X) for i in range(X)])
    after = lax.ppermute(low, "x", [(i, i - 1) for i in range(1, X)])

    channels = Y * rows // 2
    span = 2 * width
    block = jax.ShapeDtypeStruct((4, channels, span), F32)
    one = 6 * channels * span * span
    inner, outer = pl.pallas_call(
        filter_kernel,
        out_shape=(block, block),
        in_specs=[VMEM] * 2,
        out_specs=(VMEM, VMEM),
        scratch_shapes=[pltpu.VMEM((channels, Z * span), BF16)] * 2
        + [pltpu.VMEM(((taps.shape[1] + 1) * span, span), BF16)] * 2,
        compiler_params=params(10),
        cost_estimate=cost(34 * one, 6e6),
        name="filter_inner",
    )(got, taps)
    swap = [(0, 1), (1, 0)]
    inner_other = lax.ppermute(inner, "core", swap)
    depth = 4 * span
    left = pltpu.VMEM((4 * channels, depth), BF16)
    right = pltpu.VMEM((2 * channels, depth), BF16)
    square = jax.ShapeDtypeStruct((2 * channels, channels), F32)
    unit = 6 * 2 * channels * channels * depth
    here = call(own_kernel, square, [left], unit, 3e6, "own_inner", inner)
    outer, here = lax.optimization_barrier((outer, here))
    edge = pl.pallas_call(
        edge_kernel,
        out_shape=block,
        in_specs=[SMEM] + [pl.BlockSpec(memory_space=pltpu.HBM)] * 2 + [VMEM] * 2,
        out_specs=VMEM,
        scratch_shapes=[pltpu.VMEM((channels, 2 * span), BF16)] * 4
        + [pltpu.VMEM((4 * span, span), BF16)] * 2
        + [pltpu.VMEM((2,) + border.shape, F32), pltpu.SemaphoreType.DMA((2,))],
        compiler_params=params(10),
        cost_estimate=cost(6 * one, 4e6),
        name="filter_edge",
    )(first, before, after, outer, taps)
    edge_other = lax.ppermute(edge, "core", swap)
    here_edge, there = call(
        middle_kernel, (square, square), [left, right], 2 * unit, 6e6, "other_inner", inner, inner_other, edge
    )
    group = channels // Y
    spread = jax.ShapeDtypeStruct((X, 2, 2, group, 2 * channels), F32)
    total = call(
        last_kernel, spread, [left, right], unit, 5e6, "other_edge", edge, edge_other, here, here_edge, there,
        place=at_y.astype(jnp.int32).reshape(1),
    )

    parts = lax.all_to_all(total, "x", 0, 0, tiled=True)
    piece = jax.ShapeDtypeStruct((2, group, 2 * channels), F32)
    sends = pl.pallas_call(
        functools.partial(sum_kernel, 1.0 / gate_count),
        out_shape=(piece, piece),
        in_specs=[VMEM],
        out_specs=(VMEM, VMEM),
        compiler_params=params(4),
        cost_estimate=cost(1e6, 2e6),
        name="add_up",
    )(parts)
    got = [lax.ppermute(part, ("y", "x"), pairs) for part, pairs in zip(sends, last_sends())]
    return pl.pallas_call(
        place_kernel,
        out_shape=jax.ShapeDtypeStruct((2, 2, group, 2 * channels), F32),
        in_specs=[SMEM, VMEM, VMEM],
        out_specs=VMEM,
        compiler_params=params(4),
        cost_estimate=cost(1e5, 1e6),
        name="place",
    )(swapped, *got)


def solution(mesh):
    split = Mesh(mesh.devices.reshape(Y, CORE, X, Z), ("y", "core", "x", "z"))
    in_specs = (P(None, ("y", "core"), None, ("x", "z")), P())
    out_specs = P(None, ("x", "z"), ("y", "core"), None)
    return jax.shard_map(
        per_device, mesh=split, in_specs=in_specs, out_specs=out_specs, check_vma=False
    )
```

```python
import functools
import math

import jax
import jax.numpy as jnp
from jax import lax
from jax.experimental import pallas as pl
from jax.experimental.pallas import tpu as pltpu
from jax.sharding import Mesh
from jax.sharding import PartitionSpec as P

VMEM = pl.BlockSpec(memory_space=pltpu.VMEM)
SMEM = pl.BlockSpec(memory_space=pltpu.SMEM)
F32 = jnp.float32
BF16 = jnp.bfloat16
Y, CORE, X, Z = 8, 2, 4, 8


def halves(value):
    high = value.astype(BF16)
    return high, (value - high.astype(F32)).astype(BF16)


def dot3(left, right, dims):
    lh, ll = left
    rh, rl = right
    mul = lambda a, b: lax.dot_general(a, b, (dims, ((), ())), preferred_element_type=F32)
    return mul(lh, rh) + mul(ll, rh) + mul(lh, rl)


NN = ((1,), (0,))
NT = ((1,), (1,))


def params(mib):
    return pltpu.CompilerParams(vmem_limit_bytes=mib << 20)


def cost(flops, moved):
    return pl.CostEstimate(flops=int(flops), bytes_accessed=int(moved), transcendentals=0)


def bin_of(z, y):
    return 2 * (Z * (y % X) + z) + y // X


def doppler_table(pulses):
    shape = (2 * pulses, 2 * pulses)
    row = lax.broadcasted_iota(jnp.int32, shape, 0)
    column = lax.broadcasted_iota(jnp.int32, shape, 1)
    target = lax.shift_right_logical(row, 1)
    y, z = target & (Y - 1), lax.shift_right_logical(target, Y.bit_length() - 1)
    bins = 2 * (Z * (y & (X - 1)) + z) + lax.shift_right_logical(y, X.bit_length() - 1)
    pulse = column & (pulses - 1)
    part = lax.shift_right_logical(column, pulses.bit_length() - 1)
    steps = bins * pulse + ((row & 1) - part) * (pulses // 4) & (pulses - 1)
    table = jnp.cos(steps.astype(F32) * (2.0 * math.pi / pulses)) * (1.0 / math.sqrt(pulses))
    return halves(table)


GROUPS = 8


def doppler_kernel(x_hbm, o_ref, x_ref, sems):
    _, channels, pulses, lanes = x_ref.shape
    rows = 2 * pulses
    group = channels // GROUPS
    copies = []
    for n in range(GROUPS):
        here = pl.ds(n * group, group)
        copies.append(pltpu.make_async_copy(x_hbm.at[:, here], x_ref.at[:, here], sems.at[n]))
    copies[0].start()
    copies[1].start()
    high, low = doppler_table(pulses)
    table = jnp.concatenate(
        [jnp.concatenate([high, high], axis=1), jnp.concatenate([low, jnp.zeros_like(low)], axis=1)], axis=0
    )
    for c in range(0, channels, 2):
        n = c // group
        if c % group == 0:
            copies[n].wait()
            if n + 2 < GROUPS:
                copies[n + 2].start()
        pair = jnp.concatenate(
            [
                jnp.concatenate([x_ref[0, c], x_ref[0, c + 1]], axis=1),
                jnp.concatenate([x_ref[1, c], x_ref[1, c + 1]], axis=1),
            ],
            axis=0,
        )
        both = jnp.dot(table, jnp.concatenate(halves(pair), axis=0), preferred_element_type=F32)
        out = both[:rows] + both[rows:]
        o_ref[pl.ds(c, rows, stride=channels), :] = out[:, :lanes]
        o_ref[pl.ds(c + 1, rows, stride=channels), :] = out[:, lanes:]


def doppler(echoes):
    _, channels, pulses, gates = echoes.shape
    rows = 2 * pulses
    return pl.pallas_call(
        doppler_kernel,
        out_shape=jax.ShapeDtypeStruct((rows * channels, gates), F32),
        in_specs=[pl.BlockSpec(memory_space=pltpu.HBM)],
        out_specs=VMEM,
        scratch_shapes=[pltpu.VMEM(echoes.shape, F32), pltpu.SemaphoreType.DMA((GROUPS,))],
        compiler_params=params(51),
        cost_estimate=cost(6 * rows * rows * channels * gates, 16 * pulses * channels * gates),
        name="doppler",
    )(echoes)


def tap_table(taps_ref, k):
    steps, width = taps_ref.shape[1:]
    zero = jnp.zeros((1, width), F32)
    block = []
    for part in range(2):
        later = taps_ref[part, k : k + 1, :] if k < steps else zero
        earlier = taps_ref[part, k - 1 : k, :] if k > 0 else zero
        line = jnp.concatenate([later, earlier], axis=1)
        turned = pltpu.roll(jnp.broadcast_to(line, (width, 2 * width)), 0, 1, stride=1, stride_axis=0)
        block.append(turned[:, :width].T)
    re, im = block
    return jnp.concatenate(
        [jnp.concatenate([re, im], axis=1), jnp.concatenate([-im, re], axis=1)], axis=0
    )


def fill_tables(taps_ref, wh_ref, wl_ref, lags):
    span = wh_ref.shape[1]
    for n, k in enumerate(lags):
        high, low = halves(tap_table(taps_ref, k))
        wh_ref[n * span : (n + 1) * span, :] = high
        wl_ref[n * span : (n + 1) * span, :] = low


def load_blocks(ref, count, high_ref, low_ref):
    rows = ref.shape[0] // count
    half = ref.shape[1] // 2
    width = ref.shape[2]
    for n in range(count):
        for part in range(2):
            piece = ref[n * rows : (n + 1) * rows, part * half : (part + 1) * half, :]
            high, low = halves(piece.reshape(rows * half, width))
            lanes = slice((2 * n + part) * width, (2 * n + part + 1) * width)
            high_ref[:, lanes] = high
            low_ref[:, lanes] = low


def filter_kernel(x_ref, taps_ref, inner_ref, outer_ref, high, low, wh_ref, wl_ref):
    span = wh_ref.shape[1]
    fill_tables(taps_ref, wh_ref, wl_ref, range(taps_ref.shape[1] + 1))
    blocks = Z
    load_blocks(x_ref, blocks, high, low)

    def term(first, last, lag):
        lanes = slice(first * span, last * span)
        rows = slice(lag * span, (lag + last - first) * span)
        return dot3((high[:, lanes], low[:, lanes]), (wh_ref[rows, :], wl_ref[rows, :]), NN)

    for j in range(4):
        inner_ref[j] = term(j, j + 5, 0)
    outer_ref[0] = term(0, 3, 2)
    outer_ref[1] = term(0, 4, 1)
    outer_ref[2] = term(4, 8, 0)
    outer_ref[3] = term(5, 8, 0)


def edge_kernel(
    first_ref, before_hbm, after_hbm, outer_ref, taps_ref, o_ref, bh, bl, ah, al, wh_ref, wl_ref, borders, sems
):
    span = wh_ref.shape[1]
    lags = taps_ref.shape[1]
    copies = [
        pltpu.make_async_copy(source, borders.at[n], sems.at[n]) for n, source in enumerate((before_hbm, after_hbm))
    ]
    for copy in copies:
        copy.start()
    fill_tables(taps_ref, wh_ref, wl_ref, (0, 1, lags - 1, lags))
    copies[0].wait()
    load_blocks(borders.at[0], 2, bh, bl)
    copies[1].wait()
    load_blocks(borders.at[1], 2, ah, al)

    def term(high, low, first, last, lag):
        lanes = slice(first * span, last * span)
        rows = slice(lag * span, (lag + last - first) * span)
        return dot3((high[:, lanes], low[:, lanes]), (wh_ref[rows, :], wl_ref[rows, :]), NN)

    keep = first_ref[0] == 0
    zero = jnp.zeros(outer_ref.shape[1:], F32)
    o_ref[0] = jnp.where(keep, outer_ref[0], zero) + term(bh, bl, 0, 2, 0)
    o_ref[1] = jnp.where(keep, outer_ref[1], zero) + term(bh, bl, 1, 2, 0)
    o_ref[2] = outer_ref[2] + term(ah, al, 0, 1, 3)
    o_ref[3] = outer_ref[3] + term(ah, al, 0, 2, 2)


def left_factor(own_ref, ref):
    blocks, rows, span = own_ref.shape
    width = span // 2
    for n in range(blocks):
        lanes = slice(n * span, (n + 1) * span)
        for top, part in zip((0, 2 * rows), halves(own_ref[n])):
            ref[top : top + rows, lanes] = part
            ref[top + rows : top + 2 * rows, lanes] = jnp.concatenate(
                [part[:, width:], -part[:, :width]], axis=1
            )


def right_factor(other_ref, ref):
    blocks, rows, span = other_ref.shape
    for n in range(blocks):
        for top, part in zip((0, rows), halves(other_ref[n])):
            ref[top : top + rows, n * span : (n + 1) * span] = part


def product(left, right):
    rows = left.shape[0] // 4
    mul = lambda a, b: lax.dot_general(a, b, (NT, ((), ())), preferred_element_type=F32)
    high = left[:rows, :] if right is None else right[:rows, :]
    low = left[2 * rows : 3 * rows, :] if right is None else right[rows:, :]
    both = mul(left[...], high)
    return both[: 2 * rows] + both[2 * rows :] + mul(left[: 2 * rows, :], low)


def own_kernel(own_ref, o_ref, left):
    left_factor(own_ref, left)
    o_ref[...] = product(left, None)


def middle_kernel(own_ref, other_ref, edge_ref, here_ref, there_ref, left, right):
    left_factor(own_ref, left)
    right_factor(other_ref, right)
    there_ref[...] = product(left, right)
    left_factor(edge_ref, left)
    here_ref[...] = product(left, None)


def last_kernel(place_ref, own_ref, other_ref, before_ref, here_ref, there_ref, o_ref, left, right):
    left_factor(own_ref, left)
    right_factor(other_ref, right)
    there = there_ref[...] + product(left, right)
    rows = here_ref.shape[1]
    group = rows // Y
    for y in range(Y):
        x, turn = handed_to(y, place_ref[0])
        for part in range(2):
            start = part * rows + y * group
            here = slice(start, start + group)
            o_ref[x, turn, part, :, :rows] = before_ref[here, :] + here_ref[here, :]
            o_ref[x, turn, part, :, rows:] = there[start : start + group]


def handed_to(y, at_y):
    ahead = lax.rem(y - at_y + Y, Y)
    pair = lax.div(lax.rem(ahead + 1, Y), 2)
    x = lax.rem(at_y + 2 - pair + X, X)
    turn = lax.rem(ahead + 1 + lax.div(at_y, X), 2)
    return x, turn


def last_sends():
    sends = [[], []]
    for at_y in range(Y):
        for y in range(Y):
            ahead = (y - at_y) % Y
            x = (at_y + 2 - (ahead + 1) % Y // 2) % X
            turn = (ahead + 1 + at_y // X) % 2
            sends[turn].append((at_y * X + x, y * X + at_y % X))
    return sends


def call(kernel, out_shape, scratch, flops, moved, name, *operands, place=None):
    scalars = [] if place is None else [place]
    return pl.pallas_call(
        kernel,
        out_shape=out_shape,
        in_specs=[SMEM] * len(scalars) + [VMEM] * len(operands),
        out_specs=jax.tree.map(lambda _: VMEM, out_shape),
        scratch_shapes=scratch,
        compiler_params=params(12),
        cost_estimate=cost(flops, moved),
        name=name,
    )(*scalars, *operands)


def sum_kernel(scale, parts_ref, first_ref, second_ref):
    for turn, out in enumerate((first_ref, second_ref)):
        total = parts_ref[0, turn]
        for x in range(1, X):
            total = total + parts_ref[x, turn]
        out[...] = total * scale


def in_order(source, part, side):
    rows = source.shape[2] // 2
    group = rows // Y
    tile = 4 * group
    lane = lax.broadcasted_iota(jnp.int32, (source.shape[1], tile), 1)
    odd, late = (lane & group) != 0, lane >= 2 * group
    own, other = source[part, :, :rows], source[part, :, rows:]
    low, high = jnp.where(side == 0, own, other), jnp.where(side == 0, other, own)
    for y in range(0, Y, 2):
        here = slice(y * group // tile * tile, y * group // tile * tile + tile)
        ahead = y * group % tile
        turned = [
            pltpu.roll(values[:, here], (n * group - ahead - n // 2 * group) % tile, 1)
            for n, values in enumerate((low, high, low, high))
        ]
        pair = [jnp.where(odd, turned[n + 1], turned[n]) for n in (0, 2)]
        yield slice(2 * y * group, 2 * y * group + tile), jnp.where(late, pair[1], pair[0])


def order_kernel(swap_ref, first_ref, o_ref):
    for part in range(2):
        for here, values in in_order(first_ref, part, swap_ref[1]):
            o_ref[part, :, here] = values


def place_kernel(swap_ref, first_ref, second_ref, o_ref):
    swap = swap_ref[0]
    for part in range(2):
        o_ref[part, swap] = first_ref[part]
        for here, values in in_order(second_ref, part, swap_ref[1]):
            o_ref[part, 1 - swap, :, here] = values


def border_kernel(x_ref, low_ref, high_ref, sems):
    count = low_ref.shape[0]
    copies = [
        pltpu.make_async_copy(x_ref.at[pl.ds(start, count)], out, sems.at[n])
        for n, (start, out) in enumerate(((0, low_ref), (x_ref.shape[0] - count, high_ref)))
    ]
    for copy in copies:
        copy.start()
    for copy in copies:
        copy.wait()


def per_device(echoes, filter_taps):
    width = echoes.shape[3]
    pulses = echoes.shape[2]
    gate_count = width * X * Z
    at_x, at_y = lax.axis_index("x"), lax.axis_index("y")
    first = (at_x == 0).astype(jnp.int32).reshape(1)
    swapped = jnp.stack([at_y + at_x + 1 & 1, lax.axis_index("core")]).astype(jnp.int32)

    sent = doppler(echoes)
    taps = filter_taps.reshape(2, -1, width)
    rows = 2 * echoes.shape[1]
    got = lax.all_to_all(sent.reshape(pulses, rows, width), ("z", "y"), 0, 0, tiled=True)
    border = jax.ShapeDtypeStruct((2 * Y, rows, width), F32)
    low, high = pl.pallas_call(
        border_kernel,
        out_shape=(border, border),
        in_specs=[VMEM],
        out_specs=(pl.BlockSpec(memory_space=pltpu.HBM),) * 2,
        scratch_shapes=[pltpu.SemaphoreType.DMA((2,))],
        compiler_params=params(2),
        cost_estimate=cost(1e4, 2e6),
        name="borders",
    )(got)
    before = lax.ppermute(high, "x", [(i, (i + 1) % X) for i in range(X)])
    after = lax.ppermute(low, "x", [(i, i - 1) for i in range(1, X)])

    channels = Y * rows // 2
    span = 2 * width
    block = jax.ShapeDtypeStruct((4, channels, span), F32)
    one = 6 * channels * span * span
    inner, outer = pl.pallas_call(
        filter_kernel,
        out_shape=(block, block),
        in_specs=[VMEM] * 2,
        out_specs=(VMEM, VMEM),
        scratch_shapes=[pltpu.VMEM((channels, Z * span), BF16)] * 2
        + [pltpu.VMEM(((taps.shape[1] + 1) * span, span), BF16)] * 2,
        compiler_params=params(10),
        cost_estimate=cost(34 * one, 6e6),
        name="filter_inner",
    )(got, taps)
    swap = [(0, 1), (1, 0)]
    inner_other = lax.ppermute(inner, "core", swap)
    depth = 4 * span
    left = pltpu.VMEM((4 * channels, depth), BF16)
    right = pltpu.VMEM((2 * channels, depth), BF16)
    square = jax.ShapeDtypeStruct((2 * channels, channels), F32)
    unit = 6 * 2 * channels * channels * depth
    here = call(own_kernel, square, [left], unit, 3e6, "own_inner", inner)
    outer, here = lax.optimization_barrier((outer, here))
    edge = pl.pallas_call(
        edge_kernel,
        out_shape=block,
        in_specs=[SMEM] + [pl.BlockSpec(memory_space=pltpu.HBM)] * 2 + [VMEM] * 2,
        out_specs=VMEM,
        scratch_shapes=[pltpu.VMEM((channels, 2 * span), BF16)] * 4
        + [pltpu.VMEM((4 * span, span), BF16)] * 2
        + [pltpu.VMEM((2,) + border.shape, F32), pltpu.SemaphoreType.DMA((2,))],
        compiler_params=params(10),
        cost_estimate=cost(6 * one, 4e6),
        name="filter_edge",
    )(first, before, after, outer, taps)
    edge_other = lax.ppermute(edge, "core", swap)
    here_edge, there = call(
        middle_kernel, (square, square), [left, right], 2 * unit, 6e6, "other_inner", inner, inner_other, edge
    )
    group = channels // Y
    spread = jax.ShapeDtypeStruct((X, 2, 2, group, 2 * channels), F32)
    total = call(
        last_kernel, spread, [left, right], unit, 5e6, "other_edge", edge, edge_other, here, here_edge, there,
        place=at_y.astype(jnp.int32).reshape(1),
    )

    parts = lax.all_to_all(total, "x", 0, 0, tiled=True)
    piece = jax.ShapeDtypeStruct((2, group, 2 * channels), F32)
    sends = pl.pallas_call(
        functools.partial(sum_kernel, 1.0 / gate_count),
        out_shape=(piece, piece),
        in_specs=[VMEM],
        out_specs=(VMEM, VMEM),
        compiler_params=params(4),
        cost_estimate=cost(1e6, 2e6),
        name="add_up",
    )(parts)
    got = [lax.ppermute(part, ("y", "x"), pairs) for part, pairs in zip(sends, last_sends())]
    ready = pl.pallas_call(
        order_kernel,
        out_shape=piece,
        in_specs=[SMEM, VMEM],
        out_specs=VMEM,
        compiler_params=params(4),
        cost_estimate=cost(1e5, 5e5),
        name="order",
    )(swapped, got[0])
    return pl.pallas_call(
        place_kernel,
        out_shape=jax.ShapeDtypeStruct((2, 2, group, 2 * channels), F32),
        in_specs=[SMEM, VMEM, VMEM],
        out_specs=VMEM,
        compiler_params=params(4),
        cost_estimate=cost(1e5, 1e6),
        name="place",
    )(swapped, ready, got[1])


def solution(mesh):
    split = Mesh(mesh.devices.reshape(Y, CORE, X, Z), ("y", "core", "x", "z"))
    in_specs = (P(None, ("y", "core"), None, ("x", "z")), P())
    out_specs = P(None, ("x", "z"), ("y", "core"), None)
    return jax.shard_map(
        per_device, mesh=split, in_specs=in_specs, out_specs=out_specs, check_vma=False
    )
```

```python
import functools
import math

import jax
import jax.numpy as jnp
from jax import lax
from jax.experimental import pallas as pl
from jax.experimental.pallas import tpu as pltpu
from jax.sharding import Mesh
from jax.sharding import PartitionSpec as P

VMEM = pl.BlockSpec(memory_space=pltpu.VMEM)
SMEM = pl.BlockSpec(memory_space=pltpu.SMEM)
F32 = jnp.float32
BF16 = jnp.bfloat16
Y, CORE, X, Z = 8, 2, 4, 8


def halves(value):
    high = value.astype(BF16)
    return high, (value - high.astype(F32)).astype(BF16)


def dot3(left, right, dims):
    lh, ll = left
    rh, rl = right
    mul = lambda a, b: lax.dot_general(a, b, (dims, ((), ())), preferred_element_type=F32)
    return mul(lh, rh) + mul(ll, rh) + mul(lh, rl)


NN = ((1,), (0,))
NT = ((1,), (1,))


def params(mib):
    return pltpu.CompilerParams(vmem_limit_bytes=mib << 20)


def cost(flops, moved):
    return pl.CostEstimate(flops=int(flops), bytes_accessed=int(moved), transcendentals=0)


def bin_of(z, y):
    return 2 * (Z * (y % X) + z) + y // X


def doppler_table(pulses):
    shape = (2 * pulses, 2 * pulses)
    row = lax.broadcasted_iota(jnp.int32, shape, 0)
    column = lax.broadcasted_iota(jnp.int32, shape, 1)
    target = lax.shift_right_logical(row, 1)
    y, z = target & (Y - 1), lax.shift_right_logical(target, Y.bit_length() - 1)
    bins = 2 * (Z * (y & (X - 1)) + z) + lax.shift_right_logical(y, X.bit_length() - 1)
    pulse = column & (pulses - 1)
    part = lax.shift_right_logical(column, pulses.bit_length() - 1)
    steps = bins * pulse + ((row & 1) - part) * (pulses // 4) & (pulses - 1)
    table = jnp.cos(steps.astype(F32) * (2.0 * math.pi / pulses)) * (1.0 / math.sqrt(pulses))
    return halves(table)


GROUPS = 2


def doppler_kernel(x_hbm, o_ref, x_ref, sems):
    _, channels, pulses, lanes = x_ref.shape
    rows = 2 * pulses
    group = channels // GROUPS
    copies = []
    for n in range(GROUPS):
        here = pl.ds(n * group, group)
        copies.append(pltpu.make_async_copy(x_hbm.at[:, here], x_ref.at[:, here], sems.at[n]))
        copies[-1].start()
    table = doppler_table(pulses)
    for c in range(0, channels, 2):
        if c % group == 0:
            copies[c // group].wait()
        pair = jnp.concatenate(
            [
                jnp.concatenate([x_ref[0, c], x_ref[0, c + 1]], axis=1),
                jnp.concatenate([x_ref[1, c], x_ref[1, c + 1]], axis=1),
            ],
            axis=0,
        )
        out = dot3(table, halves(pair), NN)
        o_ref[pl.ds(c, rows, stride=channels), :] = out[:, :lanes]
        o_ref[pl.ds(c + 1, rows, stride=channels), :] = out[:, lanes:]


def doppler(echoes):
    _, channels, pulses, gates = echoes.shape
    rows = 2 * pulses
    return pl.pallas_call(
        doppler_kernel,
        out_shape=jax.ShapeDtypeStruct((rows * channels, gates), F32),
        in_specs=[pl.BlockSpec(memory_space=pltpu.HBM)],
        out_specs=VMEM,
        scratch_shapes=[pltpu.VMEM(echoes.shape, F32), pltpu.SemaphoreType.DMA((GROUPS,))],
        compiler_params=params(51),
        cost_estimate=cost(6 * rows * rows * channels * gates, 16 * pulses * channels * gates),
        name="doppler",
    )(echoes)


def tap_table(taps_ref, k):
    steps, width = taps_ref.shape[1:]
    zero = jnp.zeros((1, width), F32)
    block = []
    for part in range(2):
        later = taps_ref[part, k : k + 1, :] if k < steps else zero
        earlier = taps_ref[part, k - 1 : k, :] if k > 0 else zero
        line = jnp.concatenate([later, earlier], axis=1)
        turned = pltpu.roll(jnp.broadcast_to(line, (width, 2 * width)), 0, 1, stride=1, stride_axis=0)
        block.append(turned[:, :width].T)
    re, im = block
    return jnp.concatenate(
        [jnp.concatenate([re, im], axis=1), jnp.concatenate([-im, re], axis=1)], axis=0
    )


def fill_tables(taps_ref, wh_ref, wl_ref, lags):
    span = wh_ref.shape[1]
    for n, k in enumerate(lags):
        high, low = halves(tap_table(taps_ref, k))
        wh_ref[n * span : (n + 1) * span, :] = high
        wl_ref[n * span : (n + 1) * span, :] = low


def load_blocks(ref, count, high_ref, low_ref):
    rows = ref.shape[0] // count
    half = ref.shape[1] // 2
    width = ref.shape[2]
    for n in range(count):
        for part in range(2):
            piece = ref[n * rows : (n + 1) * rows, part * half : (part + 1) * half, :]
            high, low = halves(piece.reshape(rows * half, width))
            lanes = slice((2 * n + part) * width, (2 * n + part + 1) * width)
            high_ref[:, lanes] = high
            low_ref[:, lanes] = low


def filter_kernel(x_ref, taps_ref, inner_ref, outer_ref, high, low, wh_ref, wl_ref):
    span = wh_ref.shape[1]
    fill_tables(taps_ref, wh_ref, wl_ref, range(taps_ref.shape[1] + 1))
    blocks = Z
    load_blocks(x_ref, blocks, high, low)

    def term(first, last, lag):
        lanes = slice(first * span, last * span)
        rows = slice(lag * span, (lag + last - first) * span)
        return dot3((high[:, lanes], low[:, lanes]), (wh_ref[rows, :], wl_ref[rows, :]), NN)

    for j in range(4):
        inner_ref[j] = term(j, j + 5, 0)
    outer_ref[0] = term(0, 3, 2)
    outer_ref[1] = term(0, 4, 1)
    outer_ref[2] = term(4, 8, 0)
    outer_ref[3] = term(5, 8, 0)


def edge_kernel(
    first_ref, before_hbm, after_hbm, outer_ref, taps_ref, o_ref, bh, bl, ah, al, wh_ref, wl_ref, borders, sems
):
    span = wh_ref.shape[1]
    lags = taps_ref.shape[1]
    copies = [
        pltpu.make_async_copy(source, borders.at[n], sems.at[n]) for n, source in enumerate((before_hbm, after_hbm))
    ]
    for copy in copies:
        copy.start()
    fill_tables(taps_ref, wh_ref, wl_ref, (0, 1, lags - 1, lags))
    copies[0].wait()
    load_blocks(borders.at[0], 2, bh, bl)
    copies[1].wait()
    load_blocks(borders.at[1], 2, ah, al)

    def term(high, low, first, last, lag):
        lanes = slice(first * span, last * span)
        rows = slice(lag * span, (lag + last - first) * span)
        return dot3((high[:, lanes], low[:, lanes]), (wh_ref[rows, :], wl_ref[rows, :]), NN)

    keep = first_ref[0] == 0
    zero = jnp.zeros(outer_ref.shape[1:], F32)
    o_ref[0] = jnp.where(keep, outer_ref[0], zero) + term(bh, bl, 0, 2, 0)
    o_ref[1] = jnp.where(keep, outer_ref[1], zero) + term(bh, bl, 1, 2, 0)
    o_ref[2] = outer_ref[2] + term(ah, al, 0, 1, 3)
    o_ref[3] = outer_ref[3] + term(ah, al, 0, 2, 2)


def left_factor(own_ref, ref):
    blocks, rows, span = own_ref.shape
    width = span // 2
    for n in range(blocks):
        lanes = slice(n * span, (n + 1) * span)
        for top, part in zip((0, 2 * rows), halves(own_ref[n])):
            ref[top : top + rows, lanes] = part
            ref[top + rows : top + 2 * rows, lanes] = jnp.concatenate(
                [part[:, width:], -part[:, :width]], axis=1
            )


def right_factor(other_ref, ref):
    blocks, rows, span = other_ref.shape
    for n in range(blocks):
        for top, part in zip((0, rows), halves(other_ref[n])):
            ref[top : top + rows, n * span : (n + 1) * span] = part


def product(left, right):
    rows = left.shape[0] // 4
    mul = lambda a, b: lax.dot_general(a, b, (NT, ((), ())), preferred_element_type=F32)
    high = left[:rows, :] if right is None else right[:rows, :]
    low = left[2 * rows : 3 * rows, :] if right is None else right[rows:, :]
    both = mul(left[...], high)
    return both[: 2 * rows] + both[2 * rows :] + mul(left[: 2 * rows, :], low)


def own_kernel(own_ref, o_ref, left):
    left_factor(own_ref, left)
    o_ref[...] = product(left, None)


def middle_kernel(own_ref, other_ref, edge_ref, here_ref, there_ref, left, right):
    left_factor(own_ref, left)
    right_factor(other_ref, right)
    there_ref[...] = product(left, right)
    left_factor(edge_ref, left)
    here_ref[...] = product(left, None)


def last_kernel(place_ref, own_ref, other_ref, before_ref, here_ref, there_ref, o_ref, left, right):
    left_factor(own_ref, left)
    right_factor(other_ref, right)
    there = there_ref[...] + product(left, right)
    rows = here_ref.shape[1]
    group = rows // Y
    for y in range(Y):
        x, turn = handed_to(y, place_ref[0])
        for part in range(2):
            start = part * rows + y * group
            here = slice(start, start + group)
            o_ref[x, turn, part, :, :rows] = before_ref[here, :] + here_ref[here, :]
            o_ref[x, turn, part, :, rows:] = there[start : start + group]


def handed_to(y, at_y):
    ahead = lax.rem(y - at_y + Y, Y)
    pair = lax.div(lax.rem(ahead + 1, Y), 2)
    x = lax.rem(at_y + 2 - pair + X, X)
    turn = lax.rem(ahead + 1 + lax.div(at_y, X), 2)
    return x, turn


def last_sends():
    sends = [[], []]
    for at_y in range(Y):
        for y in range(Y):
            ahead = (y - at_y) % Y
            x = (at_y + 2 - (ahead + 1) % Y // 2) % X
            turn = (ahead + 1 + at_y // X) % 2
            sends[turn].append((at_y * X + x, y * X + at_y % X))
    return sends


def call(kernel, out_shape, scratch, flops, moved, name, *operands, place=None):
    scalars = [] if place is None else [place]
    return pl.pallas_call(
        kernel,
        out_shape=out_shape,
        in_specs=[SMEM] * len(scalars) + [VMEM] * len(operands),
        out_specs=jax.tree.map(lambda _: VMEM, out_shape),
        scratch_shapes=scratch,
        compiler_params=params(12),
        cost_estimate=cost(flops, moved),
        name=name,
    )(*scalars, *operands)


def sum_kernel(scale, parts_ref, first_ref, second_ref):
    for turn, out in enumerate((first_ref, second_ref)):
        total = parts_ref[0, turn]
        for x in range(1, X):
            total = total + parts_ref[x, turn]
        out[...] = total * scale


def place_kernel(swap_ref, first_ref, second_ref, o_ref):
    swap, side = swap_ref[0], swap_ref[1]
    rows = o_ref.shape[3] // 2
    group = rows // Y
    tile = 4 * group
    lane = lax.broadcasted_iota(jnp.int32, (o_ref.shape[2], tile), 1)
    odd, late = (lane & group) != 0, lane >= 2 * group
    for source, place in ((first_ref, swap), (second_ref, 1 - swap)):
        for part in range(2):
            own, other = source[part, :, :rows], source[part, :, rows:]
            low, high = jnp.where(side == 0, own, other), jnp.where(side == 0, other, own)
            for y in range(0, Y, 2):
                here = slice(y * group // tile * tile, y * group // tile * tile + tile)
                ahead = y * group % tile
                turned = [
                    pltpu.roll(values[:, here], (n * group - ahead - n // 2 * group) % tile, 1)
                    for n, values in enumerate((low, high, low, high))
                ]
                pair = [jnp.where(odd, turned[n + 1], turned[n]) for n in (0, 2)]
                o_ref[part, place, :, 2 * y * group : 2 * y * group + tile] = jnp.where(late, pair[1], pair[0])


def border_kernel(x_ref, low_ref, high_ref, sems):
    count = low_ref.shape[0]
    copies = [
        pltpu.make_async_copy(x_ref.at[pl.ds(start, count)], out, sems.at[n])
        for n, (start, out) in enumerate(((0, low_ref), (x_ref.shape[0] - count, high_ref)))
    ]
    for copy in copies:
        copy.start()
    for copy in copies:
        copy.wait()


def per_device(echoes, filter_taps):
    width = echoes.shape[3]
    pulses = echoes.shape[2]
    gate_count = width * X * Z
    at_x, at_y = lax.axis_index("x"), lax.axis_index("y")
    first = (at_x == 0).astype(jnp.int32).reshape(1)
    swapped = jnp.stack([at_y + at_x + 1 & 1, lax.axis_index("core")]).astype(jnp.int32)

    sent = doppler(echoes)
    taps = filter_taps.reshape(2, -1, width)
    rows = 2 * echoes.shape[1]
    got = lax.all_to_all(sent.reshape(pulses, rows, width), ("z", "y"), 0, 0, tiled=True)
    border = jax.ShapeDtypeStruct((2 * Y, rows, width), F32)
    low, high = pl.pallas_call(
        border_kernel,
        out_shape=(border, border),
        in_specs=[VMEM],
        out_specs=(pl.BlockSpec(memory_space=pltpu.HBM),) * 2,
        scratch_shapes=[pltpu.SemaphoreType.DMA((2,))],
        compiler_params=params(2),
        cost_estimate=cost(1e4, 2e6),
        name="borders",
    )(got)
    before = lax.ppermute(high, "x", [(i, (i + 1) % X) for i in range(X)])
    after = lax.ppermute(low, "x", [(i, i - 1) for i in range(1, X)])

    channels = Y * rows // 2
    span = 2 * width
    block = jax.ShapeDtypeStruct((4, channels, span), F32)
    one = 6 * channels * span * span
    inner, outer = pl.pallas_call(
        filter_kernel,
        out_shape=(block, block),
        in_specs=[VMEM] * 2,
        out_specs=(VMEM, VMEM),
        scratch_shapes=[pltpu.VMEM((channels, Z * span), BF16)] * 2
        + [pltpu.VMEM(((taps.shape[1] + 1) * span, span), BF16)] * 2,
        compiler_params=params(10),
        cost_estimate=cost(34 * one, 6e6),
        name="filter_inner",
    )(got, taps)
    swap = [(0, 1), (1, 0)]
    inner_other = lax.ppermute(inner, "core", swap)
    depth = 4 * span
    left = pltpu.VMEM((4 * channels, depth), BF16)
    right = pltpu.VMEM((2 * channels, depth), BF16)
    square = jax.ShapeDtypeStruct((2 * channels, channels), F32)
    unit = 6 * 2 * channels * channels * depth
    here = call(own_kernel, square, [left], unit, 3e6, "own_inner", inner)
    outer, here = lax.optimization_barrier((outer, here))
    edge = pl.pallas_call(
        edge_kernel,
        out_shape=block,
        in_specs=[SMEM] + [pl.BlockSpec(memory_space=pltpu.HBM)] * 2 + [VMEM] * 2,
        out_specs=VMEM,
        scratch_shapes=[pltpu.VMEM((channels, 2 * span), BF16)] * 4
        + [pltpu.VMEM((4 * span, span), BF16)] * 2
        + [pltpu.VMEM((2,) + border.shape, F32), pltpu.SemaphoreType.DMA((2,))],
        compiler_params=params(10),
        cost_estimate=cost(6 * one, 4e6),
        name="filter_edge",
    )(first, before, after, outer, taps)
    edge_other = lax.ppermute(edge, "core", swap)
    here_edge, there = call(
        middle_kernel, (square, square), [left, right], 2 * unit, 6e6, "other_inner", inner, inner_other, edge
    )
    group = channels // Y
    spread = jax.ShapeDtypeStruct((X, 2, 2, group, 2 * channels), F32)
    total = call(
        last_kernel, spread, [left, right], unit, 5e6, "other_edge", edge, edge_other, here, here_edge, there,
        place=at_y.astype(jnp.int32).reshape(1),
    )

    parts = lax.all_to_all(total, "x", 0, 0, tiled=True)
    piece = jax.ShapeDtypeStruct((2, group, 2 * channels), F32)
    sends = pl.pallas_call(
        functools.partial(sum_kernel, 1.0 / gate_count),
        out_shape=(piece, piece),
        in_specs=[VMEM],
        out_specs=(VMEM, VMEM),
        compiler_params=params(4),
        cost_estimate=cost(1e6, 2e6),
        name="add_up",
    )(parts)
    got = [lax.ppermute(part, ("y", "x"), pairs) for part, pairs in zip(sends, last_sends())]
    return pl.pallas_call(
        place_kernel,
        out_shape=jax.ShapeDtypeStruct((2, 2, group, 2 * channels), F32),
        in_specs=[SMEM, VMEM, VMEM],
        out_specs=VMEM,
        compiler_params=params(4),
        cost_estimate=cost(1e5, 1e6),
        name="place",
    )(swapped, *got)


def solution(mesh):
    split = Mesh(mesh.devices.reshape(Y, CORE, X, Z), ("y", "core", "x", "z"))
    in_specs = (P(None, ("y", "core"), None, ("x", "z")), P())
    out_specs = P(None, ("x", "z"), ("y", "core"), None)
    return jax.shard_map(
        per_device, mesh=split, in_specs=in_specs, out_specs=out_specs, check_vma=False
    )
```

```python
import functools
import math

import jax
import jax.numpy as jnp
from jax import lax
from jax.experimental import pallas as pl
from jax.experimental.pallas import tpu as pltpu
from jax.sharding import Mesh
from jax.sharding import PartitionSpec as P

VMEM = pl.BlockSpec(memory_space=pltpu.VMEM)
SMEM = pl.BlockSpec(memory_space=pltpu.SMEM)
F32 = jnp.float32
BF16 = jnp.bfloat16
Y, CORE, X, Z = 8, 2, 4, 8


def halves(value):
    high = value.astype(BF16)
    return high, (value - high.astype(F32)).astype(BF16)


def dot3(left, right, dims):
    lh, ll = left
    rh, rl = right
    mul = lambda a, b: lax.dot_general(a, b, (dims, ((), ())), preferred_element_type=F32)
    return mul(lh, rh) + mul(ll, rh) + mul(lh, rl)


NN = ((1,), (0,))
NT = ((1,), (1,))


def params(mib):
    return pltpu.CompilerParams(vmem_limit_bytes=mib << 20)


def cost(flops, moved):
    return pl.CostEstimate(flops=int(flops), bytes_accessed=int(moved), transcendentals=0)


def bin_of(z, y):
    return 2 * (Z * (y % X) + z) + y // X


def doppler_table(pulses):
    shape = (2 * pulses, 2 * pulses)
    row = lax.broadcasted_iota(jnp.int32, shape, 0)
    column = lax.broadcasted_iota(jnp.int32, shape, 1)
    target = lax.shift_right_logical(row, 1)
    y, z = target & (Y - 1), lax.shift_right_logical(target, Y.bit_length() - 1)
    bins = 2 * (Z * (y & (X - 1)) + z) + lax.shift_right_logical(y, X.bit_length() - 1)
    pulse = column & (pulses - 1)
    part = lax.shift_right_logical(column, pulses.bit_length() - 1)
    steps = bins * pulse + ((row & 1) - part) * (pulses // 4) & (pulses - 1)
    table = jnp.cos(steps.astype(F32) * (2.0 * math.pi / pulses)) * (1.0 / math.sqrt(pulses))
    return halves(table)


GROUPS = 2


def doppler_kernel(x_hbm, o_ref, x_ref, sems):
    _, channels, pulses, lanes = x_ref.shape
    rows = 2 * pulses
    group = channels // GROUPS
    copies = []
    for n in range(GROUPS):
        here = pl.ds(n * group, group)
        copies.append(pltpu.make_async_copy(x_hbm.at[:, here], x_ref.at[:, here], sems.at[n]))
        copies[-1].start()
    table = doppler_table(pulses)
    for c in range(0, channels, 2):
        if c % group == 0:
            copies[c // group].wait()
        pair = jnp.concatenate(
            [
                jnp.concatenate([x_ref[0, c], x_ref[0, c + 1]], axis=1),
                jnp.concatenate([x_ref[1, c], x_ref[1, c + 1]], axis=1),
            ],
            axis=0,
        )
        out = dot3(table, halves(pair), NN)
        o_ref[pl.ds(c, rows, stride=channels), :] = out[:, :lanes]
        o_ref[pl.ds(c + 1, rows, stride=channels), :] = out[:, lanes:]


def doppler(echoes):
    _, channels, pulses, gates = echoes.shape
    rows = 2 * pulses
    return pl.pallas_call(
        doppler_kernel,
        out_shape=jax.ShapeDtypeStruct((rows * channels, gates), F32),
        in_specs=[pl.BlockSpec(memory_space=pltpu.HBM)],
        out_specs=VMEM,
        scratch_shapes=[pltpu.VMEM(echoes.shape, F32), pltpu.SemaphoreType.DMA((GROUPS,))],
        compiler_params=params(51),
        cost_estimate=cost(6 * rows * rows * channels * gates, 16 * pulses * channels * gates),
        name="doppler",
    )(echoes)


def tap_table(taps_ref, k):
    steps, width = taps_ref.shape[1:]
    zero = jnp.zeros((1, width), F32)
    block = []
    for part in range(2):
        later = taps_ref[part, k : k + 1, :] if k < steps else zero
        earlier = taps_ref[part, k - 1 : k, :] if k > 0 else zero
        line = jnp.concatenate([later, earlier], axis=1)
        turned = pltpu.roll(jnp.broadcast_to(line, (width, 2 * width)), 0, 1, stride=1, stride_axis=0)
        block.append(turned[:, :width].T)
    re, im = block
    return jnp.concatenate(
        [jnp.concatenate([re, im], axis=1), jnp.concatenate([-im, re], axis=1)], axis=0
    )


def fill_tables(taps_ref, wh_ref, wl_ref, lags):
    span = wh_ref.shape[1]
    for n, k in enumerate(lags):
        high, low = halves(tap_table(taps_ref, k))
        wh_ref[n * span : (n + 1) * span, :] = high
        wl_ref[n * span : (n + 1) * span, :] = low


def load_blocks(ref, count, high_ref, low_ref):
    rows = ref.shape[0] // count
    half = ref.shape[1] // 2
    width = ref.shape[2]
    for n in range(count):
        for part in range(2):
            piece = ref[n * rows : (n + 1) * rows, part * half : (part + 1) * half, :]
            high, low = halves(piece.reshape(rows * half, width))
            lanes = slice((2 * n + part) * width, (2 * n + part + 1) * width)
            high_ref[:, lanes] = high
            low_ref[:, lanes] = low


def filter_kernel(x_ref, taps_ref, inner_ref, outer_ref, high, low, wh_ref, wl_ref):
    span = wh_ref.shape[1]
    fill_tables(taps_ref, wh_ref, wl_ref, range(taps_ref.shape[1] + 1))
    blocks = Z
    load_blocks(x_ref, blocks, high, low)

    def term(first, last, lag):
        lanes = slice(first * span, last * span)
        rows = slice(lag * span, (lag + last - first) * span)
        return dot3((high[:, lanes], low[:, lanes]), (wh_ref[rows, :], wl_ref[rows, :]), NN)

    for j in range(4):
        inner_ref[j] = term(j, j + 5, 0)
    outer_ref[0] = term(0, 3, 2)
    outer_ref[1] = term(0, 4, 1)
    outer_ref[2] = term(4, 8, 0)
    outer_ref[3] = term(5, 8, 0)


def edge_kernel(
    first_ref, before_hbm, after_hbm, outer_ref, taps_ref, o_ref, bh, bl, ah, al, wh_ref, wl_ref, borders, sems
):
    span = wh_ref.shape[1]
    lags = taps_ref.shape[1]
    copies = [
        pltpu.make_async_copy(source, borders.at[n], sems.at[n]) for n, source in enumerate((before_hbm, after_hbm))
    ]
    for copy in copies:
        copy.start()
    fill_tables(taps_ref, wh_ref, wl_ref, (0, 1, lags - 1, lags))
    copies[0].wait()
    load_blocks(borders.at[0], 2, bh, bl)
    copies[1].wait()
    load_blocks(borders.at[1], 2, ah, al)

    def term(high, low, first, last, lag):
        lanes = slice(first * span, last * span)
        rows = slice(lag * span, (lag + last - first) * span)
        return dot3((high[:, lanes], low[:, lanes]), (wh_ref[rows, :], wl_ref[rows, :]), NN)

    keep = first_ref[0] == 0
    zero = jnp.zeros(outer_ref.shape[1:], F32)
    o_ref[0] = jnp.where(keep, outer_ref[0], zero) + term(bh, bl, 0, 2, 0)
    o_ref[1] = jnp.where(keep, outer_ref[1], zero) + term(bh, bl, 1, 2, 0)
    o_ref[2] = outer_ref[2] + term(ah, al, 0, 1, 3)
    o_ref[3] = outer_ref[3] + term(ah, al, 0, 2, 2)


def left_factor(own_ref, ref):
    blocks, rows, span = own_ref.shape
    width = span // 2
    for n in range(blocks):
        lanes = slice(n * span, (n + 1) * span)
        for top, part in zip((0, 2 * rows), halves(own_ref[n])):
            ref[top : top + rows, lanes] = part
            ref[top + rows : top + 2 * rows, lanes] = jnp.concatenate(
                [part[:, width:], -part[:, :width]], axis=1
            )


def right_factor(other_ref, ref):
    blocks, rows, span = other_ref.shape
    for n in range(blocks):
        for top, part in zip((0, rows), halves(other_ref[n])):
            ref[top : top + rows, n * span : (n + 1) * span] = part


def product(left, right):
    rows = left.shape[0] // 4
    mul = lambda a, b: lax.dot_general(a, b, (NT, ((), ())), preferred_element_type=F32)
    high = left[:rows, :] if right is None else right[:rows, :]
    low = left[2 * rows : 3 * rows, :] if right is None else right[rows:, :]
    both = mul(left[...], high)
    return both[: 2 * rows] + both[2 * rows :] + mul(left[: 2 * rows, :], low)


def own_kernel(own_ref, o_ref, left):
    left_factor(own_ref, left)
    o_ref[...] = product(left, None)


def middle_kernel(own_ref, other_ref, edge_ref, here_ref, there_ref, left, right):
    left_factor(own_ref, left)
    right_factor(other_ref, right)
    there_ref[...] = product(left, right)
    left_factor(edge_ref, left)
    here_ref[...] = product(left, None)


def last_kernel(place_ref, own_ref, other_ref, before_ref, here_ref, there_ref, o_ref, left, right):
    left_factor(own_ref, left)
    right_factor(other_ref, right)
    there = there_ref[...] + product(left, right)
    rows = here_ref.shape[1]
    group = rows // Y
    for y in range(Y):
        x, turn = handed_to(y, place_ref[0])
        for part in range(2):
            start = part * rows + y * group
            here = slice(start, start + group)
            o_ref[x, turn, part, :, :rows] = before_ref[here, :] + here_ref[here, :]
            o_ref[x, turn, part, :, rows:] = there[start : start + group]


def handed_to(y, at_y):
    ahead = lax.rem(y - at_y + Y, Y)
    pair = lax.div(lax.rem(ahead + 1, Y), 2)
    x = lax.rem(at_y + 2 - pair + X, X)
    turn = lax.rem(ahead + 1 + lax.div(at_y, X), 2)
    return x, turn


def last_sends():
    sends = [[], []]
    for at_y in range(Y):
        for y in range(Y):
            ahead = (y - at_y) % Y
            x = (at_y + 2 - (ahead + 1) % Y // 2) % X
            turn = (ahead + 1 + at_y // X) % 2
            sends[turn].append((at_y * X + x, y * X + at_y % X))
    return sends


def call(kernel, out_shape, scratch, flops, moved, name, *operands, place=None):
    scalars = [] if place is None else [place]
    return pl.pallas_call(
        kernel,
        out_shape=out_shape,
        in_specs=[SMEM] * len(scalars) + [VMEM] * len(operands),
        out_specs=jax.tree.map(lambda _: VMEM, out_shape),
        scratch_shapes=scratch,
        compiler_params=params(12),
        cost_estimate=cost(flops, moved),
        name=name,
    )(*scalars, *operands)


def sum_kernel(scale, parts_ref, first_ref, second_ref):
    for turn, out in enumerate((first_ref, second_ref)):
        total = parts_ref[0, turn]
        for x in range(1, X):
            total = total + parts_ref[x, turn]
        out[...] = total * scale


def place_kernel(swap_ref, side_ref, first_ref, second_ref, o_ref):
    swap, side = swap_ref[0], side_ref[0]
    rows = o_ref.shape[3] // 2
    group = rows // Y
    tile = 4 * group
    lane = lax.broadcasted_iota(jnp.int32, (o_ref.shape[2], tile), 1)
    odd, late = (lane & group) != 0, lane >= 2 * group
    for source, place in ((first_ref, swap), (second_ref, 1 - swap)):
        for part in range(2):
            own, other = source[part, :, :rows], source[part, :, rows:]
            low, high = jnp.where(side == 0, own, other), jnp.where(side == 0, other, own)
            for y in range(0, Y, 2):
                here = slice(y * group // tile * tile, y * group // tile * tile + tile)
                ahead = y * group % tile
                turned = [
                    pltpu.roll(values[:, here], (n * group - ahead - n // 2 * group) % tile, 1)
                    for n, values in enumerate((low, high, low, high))
                ]
                pair = [jnp.where(odd, turned[n + 1], turned[n]) for n in (0, 2)]
                o_ref[part, place, :, 2 * y * group : 2 * y * group + tile] = jnp.where(late, pair[1], pair[0])


def border_kernel(x_ref, low_ref, high_ref, sems):
    count = low_ref.shape[0]
    copies = [
        pltpu.make_async_copy(x_ref.at[pl.ds(start, count)], out, sems.at[n])
        for n, (start, out) in enumerate(((0, low_ref), (x_ref.shape[0] - count, high_ref)))
    ]
    for copy in copies:
        copy.start()
    for copy in copies:
        copy.wait()


def per_device(echoes, filter_taps):
    width = echoes.shape[3]
    pulses = echoes.shape[2]
    gate_count = width * X * Z
    at_x, at_y = lax.axis_index("x"), lax.axis_index("y")
    first = (at_x == 0).astype(jnp.int32).reshape(1)
    swapped = (at_y + at_x + 1 & 1).astype(jnp.int32).reshape(1)
    side = lax.axis_index("core").astype(jnp.int32).reshape(1)

    sent = doppler(echoes)
    taps = filter_taps.reshape(2, -1, width)
    rows = 2 * echoes.shape[1]
    got = lax.all_to_all(sent.reshape(pulses, rows, width), ("z", "y"), 0, 0, tiled=True)
    border = jax.ShapeDtypeStruct((2 * Y, rows, width), F32)
    low, high = pl.pallas_call(
        border_kernel,
        out_shape=(border, border),
        in_specs=[VMEM],
        out_specs=(pl.BlockSpec(memory_space=pltpu.HBM),) * 2,
        scratch_shapes=[pltpu.SemaphoreType.DMA((2,))],
        compiler_params=params(2),
        cost_estimate=cost(1e4, 2e6),
        name="borders",
    )(got)
    before = lax.ppermute(high, "x", [(i, (i + 1) % X) for i in range(X)])
    after = lax.ppermute(low, "x", [(i, i - 1) for i in range(1, X)])

    channels = Y * rows // 2
    span = 2 * width
    block = jax.ShapeDtypeStruct((4, channels, span), F32)
    one = 6 * channels * span * span
    inner, outer = pl.pallas_call(
        filter_kernel,
        out_shape=(block, block),
        in_specs=[VMEM] * 2,
        out_specs=(VMEM, VMEM),
        scratch_shapes=[pltpu.VMEM((channels, Z * span), BF16)] * 2
        + [pltpu.VMEM(((taps.shape[1] + 1) * span, span), BF16)] * 2,
        compiler_params=params(10),
        cost_estimate=cost(34 * one, 6e6),
        name="filter_inner",
    )(got, taps)
    swap = [(0, 1), (1, 0)]
    inner_other = lax.ppermute(inner, "core", swap)
    depth = 4 * span
    left = pltpu.VMEM((4 * channels, depth), BF16)
    right = pltpu.VMEM((2 * channels, depth), BF16)
    square = jax.ShapeDtypeStruct((2 * channels, channels), F32)
    unit = 6 * 2 * channels * channels * depth
    here = call(own_kernel, square, [left], unit, 3e6, "own_inner", inner)
    outer, here = lax.optimization_barrier((outer, here))
    edge = pl.pallas_call(
        edge_kernel,
        out_shape=block,
        in_specs=[SMEM] + [pl.BlockSpec(memory_space=pltpu.HBM)] * 2 + [VMEM] * 2,
        out_specs=VMEM,
        scratch_shapes=[pltpu.VMEM((channels, 2 * span), BF16)] * 4
        + [pltpu.VMEM((4 * span, span), BF16)] * 2
        + [pltpu.VMEM((2,) + border.shape, F32), pltpu.SemaphoreType.DMA((2,))],
        compiler_params=params(10),
        cost_estimate=cost(6 * one, 4e6),
        name="filter_edge",
    )(first, before, after, outer, taps)
    edge_other = lax.ppermute(edge, "core", swap)
    here_edge, there = call(
        middle_kernel, (square, square), [left, right], 2 * unit, 6e6, "other_inner", inner, inner_other, edge
    )
    group = channels // Y
    spread = jax.ShapeDtypeStruct((X, 2, 2, group, 2 * channels), F32)
    total = call(
        last_kernel, spread, [left, right], unit, 5e6, "other_edge", edge, edge_other, here, here_edge, there,
        place=at_y.astype(jnp.int32).reshape(1),
    )

    parts = lax.all_to_all(total, "x", 0, 0, tiled=True)
    piece = jax.ShapeDtypeStruct((2, group, 2 * channels), F32)
    sends = pl.pallas_call(
        functools.partial(sum_kernel, 1.0 / gate_count),
        out_shape=(piece, piece),
        in_specs=[VMEM],
        out_specs=(VMEM, VMEM),
        compiler_params=params(4),
        cost_estimate=cost(1e6, 2e6),
        name="add_up",
    )(parts)
    got = [lax.ppermute(part, ("y", "x"), pairs) for part, pairs in zip(sends, last_sends())]
    return pl.pallas_call(
        place_kernel,
        out_shape=jax.ShapeDtypeStruct((2, 2, group, 2 * channels), F32),
        in_specs=[SMEM, SMEM, VMEM, VMEM],
        out_specs=VMEM,
        compiler_params=params(4),
        cost_estimate=cost(1e5, 1e6),
        name="place",
    )(swapped, side, *got)


def solution(mesh):
    split = Mesh(mesh.devices.reshape(Y, CORE, X, Z), ("y", "core", "x", "z"))
    in_specs = (P(None, ("y", "core"), None, ("x", "z")), P())
    out_specs = P(None, ("x", "z"), ("y", "core"), None)
    return jax.shard_map(
        per_device, mesh=split, in_specs=in_specs, out_specs=out_specs, check_vma=False
    )
```

```python
import functools
import math

import jax
import jax.numpy as jnp
from jax import lax
from jax.experimental import pallas as pl
from jax.experimental.pallas import tpu as pltpu
from jax.sharding import Mesh
from jax.sharding import PartitionSpec as P

VMEM = pl.BlockSpec(memory_space=pltpu.VMEM)
SMEM = pl.BlockSpec(memory_space=pltpu.SMEM)
F32 = jnp.float32
BF16 = jnp.bfloat16
Y, CORE, X, Z = 8, 2, 4, 8


def halves(value):
    high = value.astype(BF16)
    return high, (value - high.astype(F32)).astype(BF16)


def dot3(left, right, dims):
    lh, ll = left
    rh, rl = right
    mul = lambda a, b: lax.dot_general(a, b, (dims, ((), ())), preferred_element_type=F32)
    return mul(lh, rh) + mul(ll, rh) + mul(lh, rl)


NN = ((1,), (0,))
NT = ((1,), (1,))


def params(mib):
    return pltpu.CompilerParams(vmem_limit_bytes=mib << 20)


def cost(flops, moved):
    return pl.CostEstimate(flops=int(flops), bytes_accessed=int(moved), transcendentals=0)


def bin_of(z, y):
    return 2 * (Z * (y % X) + z) + y // X


def doppler_table(pulses):
    shape = (2 * pulses, 2 * pulses)
    row = lax.broadcasted_iota(jnp.int32, shape, 0)
    column = lax.broadcasted_iota(jnp.int32, shape, 1)
    target = lax.shift_right_logical(row, 1)
    y, z = target & (Y - 1), lax.shift_right_logical(target, Y.bit_length() - 1)
    bins = 2 * (Z * (y & (X - 1)) + z) + lax.shift_right_logical(y, X.bit_length() - 1)
    pulse = column & (pulses - 1)
    part = lax.shift_right_logical(column, pulses.bit_length() - 1)
    steps = bins * pulse + ((row & 1) - part) * (pulses // 4) & (pulses - 1)
    table = jnp.cos(steps.astype(F32) * (2.0 * math.pi / pulses)) * (1.0 / math.sqrt(pulses))
    return halves(table)


GROUPS = 2


def doppler_kernel(x_hbm, o_ref, x_ref, sems):
    _, channels, pulses, lanes = x_ref.shape
    rows = 2 * pulses
    group = channels // GROUPS
    copies = []
    for n in range(GROUPS):
        here = pl.ds(n * group, group)
        copies.append(pltpu.make_async_copy(x_hbm.at[:, here], x_ref.at[:, here], sems.at[n]))
        copies[-1].start()
    table = doppler_table(pulses)
    for c in range(0, channels, 2):
        if c % group == 0:
            copies[c // group].wait()
        pair = jnp.concatenate(
            [
                jnp.concatenate([x_ref[0, c], x_ref[0, c + 1]], axis=1),
                jnp.concatenate([x_ref[1, c], x_ref[1, c + 1]], axis=1),
            ],
            axis=0,
        )
        out = dot3(table, halves(pair), NN)
        o_ref[pl.ds(c, rows, stride=channels), :] = out[:, :lanes]
        o_ref[pl.ds(c + 1, rows, stride=channels), :] = out[:, lanes:]


def doppler(echoes):
    _, channels, pulses, gates = echoes.shape
    rows = 2 * pulses
    return pl.pallas_call(
        doppler_kernel,
        out_shape=jax.ShapeDtypeStruct((rows * channels, gates), F32),
        in_specs=[pl.BlockSpec(memory_space=pltpu.HBM)],
        out_specs=VMEM,
        scratch_shapes=[pltpu.VMEM(echoes.shape, F32), pltpu.SemaphoreType.DMA((GROUPS,))],
        compiler_params=params(51),
        cost_estimate=cost(6 * rows * rows * channels * gates, 16 * pulses * channels * gates),
        name="doppler",
    )(echoes)


def tap_table(taps_ref, k):
    steps, width = taps_ref.shape[1:]
    zero = jnp.zeros((1, width), F32)
    block = []
    for part in range(2):
        later = taps_ref[part, k : k + 1, :] if k < steps else zero
        earlier = taps_ref[part, k - 1 : k, :] if k > 0 else zero
        line = jnp.concatenate([later, earlier], axis=1)
        turned = pltpu.roll(jnp.broadcast_to(line, (width, 2 * width)), 0, 1, stride=1, stride_axis=0)
        block.append(turned[:, :width].T)
    re, im = block
    return jnp.concatenate(
        [jnp.concatenate([re, im], axis=1), jnp.concatenate([-im, re], axis=1)], axis=0
    )


def fill_tables(taps_ref, wh_ref, wl_ref, lags):
    span = wh_ref.shape[1]
    for n, k in enumerate(lags):
        high, low = halves(tap_table(taps_ref, k))
        wh_ref[n * span : (n + 1) * span, :] = high
        wl_ref[n * span : (n + 1) * span, :] = low


def load_blocks(ref, count, high_ref, low_ref):
    rows = ref.shape[0] // count
    half = ref.shape[1] // 2
    width = ref.shape[2]
    for n in range(count):
        for part in range(2):
            piece = ref[n * rows : (n + 1) * rows, part * half : (part + 1) * half, :]
            high, low = halves(piece.reshape(rows * half, width))
            lanes = slice((2 * n + part) * width, (2 * n + part + 1) * width)
            high_ref[:, lanes] = high
            low_ref[:, lanes] = low


def filter_kernel(x_ref, taps_ref, inner_hbm, outer_ref, high, low, wh_ref, wl_ref, inner_ref, sems):
    span = wh_ref.shape[1]
    fill_tables(taps_ref, wh_ref, wl_ref, range(taps_ref.shape[1] + 1))
    blocks = Z
    load_blocks(x_ref, blocks, high, low)

    def term(first, last, lag):
        lanes = slice(first * span, last * span)
        rows = slice(lag * span, (lag + last - first) * span)
        return dot3((high[:, lanes], low[:, lanes]), (wh_ref[rows, :], wl_ref[rows, :]), NN)

    copies = []
    for j in range(4):
        inner_ref[j] = term(j, j + 5, 0)
        copies.append(pltpu.make_async_copy(inner_ref.at[j], inner_hbm.at[j], sems.at[j]))
        copies[-1].start()
    outer_ref[0] = term(0, 3, 2)
    outer_ref[1] = term(0, 4, 1)
    outer_ref[2] = term(4, 8, 0)
    outer_ref[3] = term(5, 8, 0)
    for copy in copies:
        copy.wait()


def edge_kernel(
    first_ref, before_hbm, after_hbm, outer_ref, taps_ref, o_ref, bh, bl, ah, al, wh_ref, wl_ref, borders, sems
):
    span = wh_ref.shape[1]
    lags = taps_ref.shape[1]
    copies = [
        pltpu.make_async_copy(source, borders.at[n], sems.at[n]) for n, source in enumerate((before_hbm, after_hbm))
    ]
    for copy in copies:
        copy.start()
    fill_tables(taps_ref, wh_ref, wl_ref, (0, 1, lags - 1, lags))
    copies[0].wait()
    load_blocks(borders.at[0], 2, bh, bl)
    copies[1].wait()
    load_blocks(borders.at[1], 2, ah, al)

    def term(high, low, first, last, lag):
        lanes = slice(first * span, last * span)
        rows = slice(lag * span, (lag + last - first) * span)
        return dot3((high[:, lanes], low[:, lanes]), (wh_ref[rows, :], wl_ref[rows, :]), NN)

    keep = first_ref[0] == 0
    zero = jnp.zeros(outer_ref.shape[1:], F32)
    o_ref[0] = jnp.where(keep, outer_ref[0], zero) + term(bh, bl, 0, 2, 0)
    o_ref[1] = jnp.where(keep, outer_ref[1], zero) + term(bh, bl, 1, 2, 0)
    o_ref[2] = outer_ref[2] + term(ah, al, 0, 1, 3)
    o_ref[3] = outer_ref[3] + term(ah, al, 0, 2, 2)


def left_factor(own_ref, ref):
    blocks, rows, span = own_ref.shape
    width = span // 2
    for n in range(blocks):
        lanes = slice(n * span, (n + 1) * span)
        for top, part in zip((0, 2 * rows), halves(own_ref[n])):
            ref[top : top + rows, lanes] = part
            ref[top + rows : top + 2 * rows, lanes] = jnp.concatenate(
                [part[:, width:], -part[:, :width]], axis=1
            )


def right_factor(other_ref, ref):
    blocks, rows, span = other_ref.shape
    for n in range(blocks):
        for top, part in zip((0, rows), halves(other_ref[n])):
            ref[top : top + rows, n * span : (n + 1) * span] = part


def product(left, right):
    rows = left.shape[0] // 4
    mul = lambda a, b: lax.dot_general(a, b, (NT, ((), ())), preferred_element_type=F32)
    high = left[:rows, :] if right is None else right[:rows, :]
    low = left[2 * rows : 3 * rows, :] if right is None else right[rows:, :]
    both = mul(left[...], high)
    return both[: 2 * rows] + both[2 * rows :] + mul(left[: 2 * rows, :], low)


def own_kernel(own_ref, o_ref, left):
    left_factor(own_ref, left)
    o_ref[...] = product(left, None)


def middle_kernel(own_ref, other_ref, edge_ref, here_ref, there_ref, left, right):
    left_factor(own_ref, left)
    right_factor(other_ref, right)
    there_ref[...] = product(left, right)
    left_factor(edge_ref, left)
    here_ref[...] = product(left, None)


def last_kernel(place_ref, own_ref, other_ref, before_ref, here_ref, there_ref, o_ref, left, right):
    left_factor(own_ref, left)
    right_factor(other_ref, right)
    there = there_ref[...] + product(left, right)
    rows = here_ref.shape[1]
    group = rows // Y
    for y in range(Y):
        x, turn = handed_to(y, place_ref[0])
        for part in range(2):
            start = part * rows + y * group
            here = slice(start, start + group)
            o_ref[x, turn, part, :, :rows] = before_ref[here, :] + here_ref[here, :]
            o_ref[x, turn, part, :, rows:] = there[start : start + group]


def handed_to(y, at_y):
    ahead = lax.rem(y - at_y + Y, Y)
    pair = lax.div(lax.rem(ahead + 1, Y), 2)
    x = lax.rem(at_y + 2 - pair + X, X)
    turn = lax.rem(ahead + 1 + lax.div(at_y, X), 2)
    return x, turn


def last_sends():
    sends = [[], []]
    for at_y in range(Y):
        for y in range(Y):
            ahead = (y - at_y) % Y
            x = (at_y + 2 - (ahead + 1) % Y // 2) % X
            turn = (ahead + 1 + at_y // X) % 2
            sends[turn].append((at_y * X + x, y * X + at_y % X))
    return sends


def call(kernel, out_shape, scratch, flops, moved, name, *operands, place=None):
    scalars = [] if place is None else [place]
    return pl.pallas_call(
        kernel,
        out_shape=out_shape,
        in_specs=[SMEM] * len(scalars) + [VMEM] * len(operands),
        out_specs=jax.tree.map(lambda _: VMEM, out_shape),
        scratch_shapes=scratch,
        compiler_params=params(12),
        cost_estimate=cost(flops, moved),
        name=name,
    )(*scalars, *operands)


def sum_kernel(scale, parts_ref, first_ref, second_ref):
    for turn, out in enumerate((first_ref, second_ref)):
        total = parts_ref[0, turn]
        for x in range(1, X):
            total = total + parts_ref[x, turn]
        out[...] = total * scale


def place_kernel(swap_ref, side_ref, first_ref, second_ref, o_ref):
    swap, side = swap_ref[0], side_ref[0]
    rows = o_ref.shape[3] // 2
    group = rows // Y
    tile = 4 * group
    lane = lax.broadcasted_iota(jnp.int32, (o_ref.shape[2], tile), 1)
    odd, late = (lane & group) != 0, lane >= 2 * group
    for source, place in ((first_ref, swap), (second_ref, 1 - swap)):
        for part in range(2):
            own, other = source[part, :, :rows], source[part, :, rows:]
            low, high = jnp.where(side == 0, own, other), jnp.where(side == 0, other, own)
            for y in range(0, Y, 2):
                here = slice(y * group // tile * tile, y * group // tile * tile + tile)
                ahead = y * group % tile
                turned = [
                    pltpu.roll(values[:, here], (n * group - ahead - n // 2 * group) % tile, 1)
                    for n, values in enumerate((low, high, low, high))
                ]
                pair = [jnp.where(odd, turned[n + 1], turned[n]) for n in (0, 2)]
                o_ref[part, place, :, 2 * y * group : 2 * y * group + tile] = jnp.where(late, pair[1], pair[0])


def border_kernel(x_ref, low_ref, high_ref, sems):
    count = low_ref.shape[0]
    copies = [
        pltpu.make_async_copy(x_ref.at[pl.ds(start, count)], out, sems.at[n])
        for n, (start, out) in enumerate(((0, low_ref), (x_ref.shape[0] - count, high_ref)))
    ]
    for copy in copies:
        copy.start()
    for copy in copies:
        copy.wait()


def per_device(echoes, filter_taps):
    width = echoes.shape[3]
    pulses = echoes.shape[2]
    gate_count = width * X * Z
    at_x, at_y = lax.axis_index("x"), lax.axis_index("y")
    first = (at_x == 0).astype(jnp.int32).reshape(1)
    swapped = (at_y + at_x + 1 & 1).astype(jnp.int32).reshape(1)
    side = lax.axis_index("core").astype(jnp.int32).reshape(1)

    sent = doppler(echoes)
    taps = filter_taps.reshape(2, -1, width)
    rows = 2 * echoes.shape[1]
    got = lax.all_to_all(sent.reshape(pulses, rows, width), ("z", "y"), 0, 0, tiled=True)
    border = jax.ShapeDtypeStruct((2 * Y, rows, width), F32)
    low, high = pl.pallas_call(
        border_kernel,
        out_shape=(border, border),
        in_specs=[VMEM],
        out_specs=(pl.BlockSpec(memory_space=pltpu.HBM),) * 2,
        scratch_shapes=[pltpu.SemaphoreType.DMA((2,))],
        compiler_params=params(2),
        cost_estimate=cost(1e4, 2e6),
        name="borders",
    )(got)
    before = lax.ppermute(high, "x", [(i, (i + 1) % X) for i in range(X)])
    after = lax.ppermute(low, "x", [(i, i - 1) for i in range(1, X)])

    channels = Y * rows // 2
    span = 2 * width
    block = jax.ShapeDtypeStruct((4, channels, span), F32)
    one = 6 * channels * span * span
    inner, outer = pl.pallas_call(
        filter_kernel,
        out_shape=(block, block),
        in_specs=[VMEM] * 2,
        out_specs=(pl.BlockSpec(memory_space=pltpu.HBM), VMEM),
        scratch_shapes=[pltpu.VMEM((channels, Z * span), BF16)] * 2
        + [pltpu.VMEM(((taps.shape[1] + 1) * span, span), BF16)] * 2
        + [pltpu.VMEM(block.shape, F32), pltpu.SemaphoreType.DMA((4,))],
        compiler_params=params(10),
        cost_estimate=cost(34 * one, 6e6),
        name="filter_inner",
    )(got, taps)
    swap = [(0, 1), (1, 0)]
    inner_other = lax.ppermute(inner, "core", swap)
    depth = 4 * span
    left = pltpu.VMEM((4 * channels, depth), BF16)
    right = pltpu.VMEM((2 * channels, depth), BF16)
    square = jax.ShapeDtypeStruct((2 * channels, channels), F32)
    unit = 6 * 2 * channels * channels * depth
    here = call(own_kernel, square, [left], unit, 3e6, "own_inner", inner)
    outer, here = lax.optimization_barrier((outer, here))
    edge = pl.pallas_call(
        edge_kernel,
        out_shape=block,
        in_specs=[SMEM] + [pl.BlockSpec(memory_space=pltpu.HBM)] * 2 + [VMEM] * 2,
        out_specs=VMEM,
        scratch_shapes=[pltpu.VMEM((channels, 2 * span), BF16)] * 4
        + [pltpu.VMEM((4 * span, span), BF16)] * 2
        + [pltpu.VMEM((2,) + border.shape, F32), pltpu.SemaphoreType.DMA((2,))],
        compiler_params=params(10),
        cost_estimate=cost(6 * one, 4e6),
        name="filter_edge",
    )(first, before, after, outer, taps)
    edge_other = lax.ppermute(edge, "core", swap)
    here_edge, there = call(
        middle_kernel, (square, square), [left, right], 2 * unit, 6e6, "other_inner", inner, inner_other, edge
    )
    group = channels // Y
    spread = jax.ShapeDtypeStruct((X, 2, 2, group, 2 * channels), F32)
    total = call(
        last_kernel, spread, [left, right], unit, 5e6, "other_edge", edge, edge_other, here, here_edge, there,
        place=at_y.astype(jnp.int32).reshape(1),
    )

    parts = lax.all_to_all(total, "x", 0, 0, tiled=True)
    piece = jax.ShapeDtypeStruct((2, group, 2 * channels), F32)
    sends = pl.pallas_call(
        functools.partial(sum_kernel, 1.0 / gate_count),
        out_shape=(piece, piece),
        in_specs=[VMEM],
        out_specs=(VMEM, VMEM),
        compiler_params=params(4),
        cost_estimate=cost(1e6, 2e6),
        name="add_up",
    )(parts)
    got = [lax.ppermute(part, ("y", "x"), pairs) for part, pairs in zip(sends, last_sends())]
    return pl.pallas_call(
        place_kernel,
        out_shape=jax.ShapeDtypeStruct((2, 2, group, 2 * channels), F32),
        in_specs=[SMEM, SMEM, VMEM, VMEM],
        out_specs=VMEM,
        compiler_params=params(4),
        cost_estimate=cost(1e5, 1e6),
        name="place",
    )(swapped, side, *got)


def solution(mesh):
    split = Mesh(mesh.devices.reshape(Y, CORE, X, Z), ("y", "core", "x", "z"))
    in_specs = (P(None, ("y", "core"), None, ("x", "z")), P())
    out_specs = P(None, ("x", "z"), ("y", "core"), None)
    return jax.shard_map(
        per_device, mesh=split, in_specs=in_specs, out_specs=out_specs, check_vma=False
    )
```

```python
import functools
import math

import jax
import jax.numpy as jnp
from jax import lax
from jax.experimental import pallas as pl
from jax.experimental.pallas import tpu as pltpu
from jax.sharding import Mesh
from jax.sharding import PartitionSpec as P

VMEM = pl.BlockSpec(memory_space=pltpu.VMEM)
SMEM = pl.BlockSpec(memory_space=pltpu.SMEM)
F32 = jnp.float32
BF16 = jnp.bfloat16
Y, CORE, X, Z = 8, 2, 4, 8


def halves(value):
    high = value.astype(BF16)
    return high, (value - high.astype(F32)).astype(BF16)


def dot3(left, right, dims):
    lh, ll = left
    rh, rl = right
    mul = lambda a, b: lax.dot_general(a, b, (dims, ((), ())), preferred_element_type=F32)
    return mul(lh, rh) + mul(ll, rh) + mul(lh, rl)


NN = ((1,), (0,))
NT = ((1,), (1,))


def params(mib):
    return pltpu.CompilerParams(vmem_limit_bytes=mib << 20)


def cost(flops, moved):
    return pl.CostEstimate(flops=int(flops), bytes_accessed=int(moved), transcendentals=0)


def bin_of(z, y):
    return 2 * (Z * (y % X) + z) + y // X


def doppler_table(pulses):
    shape = (2 * pulses, 2 * pulses)
    row = lax.broadcasted_iota(jnp.int32, shape, 0)
    column = lax.broadcasted_iota(jnp.int32, shape, 1)
    target = lax.shift_right_logical(row, 1)
    y, z = target & (Y - 1), lax.shift_right_logical(target, Y.bit_length() - 1)
    bins = 2 * (Z * (y & (X - 1)) + z) + lax.shift_right_logical(y, X.bit_length() - 1)
    pulse = column & (pulses - 1)
    part = lax.shift_right_logical(column, pulses.bit_length() - 1)
    steps = bins * pulse + ((row & 1) - part) * (pulses // 4) & (pulses - 1)
    table = jnp.cos(steps.astype(F32) * (2.0 * math.pi / pulses)) * (1.0 / math.sqrt(pulses))
    return halves(table)


GROUPS = 2


def doppler_kernel(x_hbm, o_ref, x_ref, sems):
    _, channels, pulses, lanes = x_ref.shape
    rows = 2 * pulses
    group = channels // GROUPS
    copies = []
    for n in range(GROUPS):
        here = pl.ds(n * group, group)
        copies.append(pltpu.make_async_copy(x_hbm.at[:, here], x_ref.at[:, here], sems.at[n]))
        copies[-1].start()
    table = doppler_table(pulses)
    for c in range(0, channels, 2):
        if c % group == 0:
            copies[c // group].wait()
        pair = jnp.concatenate(
            [
                jnp.concatenate([x_ref[0, c], x_ref[0, c + 1]], axis=1),
                jnp.concatenate([x_ref[1, c], x_ref[1, c + 1]], axis=1),
            ],
            axis=0,
        )
        out = dot3(table, halves(pair), NN)
        o_ref[pl.ds(c, rows, stride=channels), :] = out[:, :lanes]
        o_ref[pl.ds(c + 1, rows, stride=channels), :] = out[:, lanes:]


def doppler(echoes):
    _, channels, pulses, gates = echoes.shape
    rows = 2 * pulses
    return pl.pallas_call(
        doppler_kernel,
        out_shape=jax.ShapeDtypeStruct((rows * channels, gates), F32),
        in_specs=[pl.BlockSpec(memory_space=pltpu.HBM)],
        out_specs=VMEM,
        scratch_shapes=[pltpu.VMEM(echoes.shape, F32), pltpu.SemaphoreType.DMA((GROUPS,))],
        compiler_params=params(51),
        cost_estimate=cost(6 * rows * rows * channels * gates, 16 * pulses * channels * gates),
        name="doppler",
    )(echoes)


def tap_table(taps_ref, k):
    steps, width = taps_ref.shape[1:]
    zero = jnp.zeros((1, width), F32)
    block = []
    for part in range(2):
        later = taps_ref[part, k : k + 1, :] if k < steps else zero
        earlier = taps_ref[part, k - 1 : k, :] if k > 0 else zero
        line = jnp.concatenate([later, earlier], axis=1)
        turned = pltpu.roll(jnp.broadcast_to(line, (width, 2 * width)), 0, 1, stride=1, stride_axis=0)
        block.append(turned[:, :width].T)
    re, im = block
    return jnp.concatenate(
        [jnp.concatenate([re, im], axis=1), jnp.concatenate([-im, re], axis=1)], axis=0
    )


def fill_tables(taps_ref, wh_ref, wl_ref, lags):
    span = wh_ref.shape[1]
    for n, k in enumerate(lags):
        high, low = halves(tap_table(taps_ref, k))
        wh_ref[n * span : (n + 1) * span, :] = high
        wl_ref[n * span : (n + 1) * span, :] = low


def load_blocks(ref, count, high_ref, low_ref):
    rows = ref.shape[0] // count
    half = ref.shape[1] // 2
    width = ref.shape[2]
    for n in range(count):
        for part in range(2):
            piece = ref[n * rows : (n + 1) * rows, part * half : (part + 1) * half, :]
            high, low = halves(piece.reshape(rows * half, width))
            lanes = slice((2 * n + part) * width, (2 * n + part + 1) * width)
            high_ref[:, lanes] = high
            low_ref[:, lanes] = low


def filter_kernel(x_ref, taps_ref, inner_hbm, outer_ref, high, low, wh_ref, wl_ref, inner_ref, sems):
    span = wh_ref.shape[1]
    fill_tables(taps_ref, wh_ref, wl_ref, range(taps_ref.shape[1] + 1))
    blocks = Z
    load_blocks(x_ref, blocks, high, low)

    def term(first, last, lag):
        lanes = slice(first * span, last * span)
        rows = slice(lag * span, (lag + last - first) * span)
        return dot3((high[:, lanes], low[:, lanes]), (wh_ref[rows, :], wl_ref[rows, :]), NN)

    copies = []
    for j in range(4):
        inner_ref[j] = term(j, j + 5, 0)
        copies.append(pltpu.make_async_copy(inner_ref.at[j], inner_hbm.at[j], sems.at[j]))
        copies[-1].start()
    outer_ref[0] = term(0, 3, 2)
    outer_ref[1] = term(0, 4, 1)
    outer_ref[2] = term(4, 8, 0)
    outer_ref[3] = term(5, 8, 0)
    for copy in copies:
        copy.wait()


def edge_kernel(
    first_ref, before_hbm, after_hbm, outer_ref, taps_ref, o_ref, bh, bl, ah, al, wh_ref, wl_ref, borders, sems
):
    span = wh_ref.shape[1]
    lags = taps_ref.shape[1]
    copies = [
        pltpu.make_async_copy(source, borders.at[n], sems.at[n]) for n, source in enumerate((before_hbm, after_hbm))
    ]
    for copy in copies:
        copy.start()
    fill_tables(taps_ref, wh_ref, wl_ref, (0, 1, lags - 1, lags))
    copies[0].wait()
    load_blocks(borders.at[0], 2, bh, bl)
    copies[1].wait()
    load_blocks(borders.at[1], 2, ah, al)

    def term(high, low, first, last, lag):
        lanes = slice(first * span, last * span)
        rows = slice(lag * span, (lag + last - first) * span)
        return dot3((high[:, lanes], low[:, lanes]), (wh_ref[rows, :], wl_ref[rows, :]), NN)

    keep = first_ref[0] == 0
    zero = jnp.zeros(outer_ref.shape[1:], F32)
    o_ref[0] = jnp.where(keep, outer_ref[0], zero) + term(bh, bl, 0, 2, 0)
    o_ref[1] = jnp.where(keep, outer_ref[1], zero) + term(bh, bl, 1, 2, 0)
    o_ref[2] = outer_ref[2] + term(ah, al, 0, 1, 3)
    o_ref[3] = outer_ref[3] + term(ah, al, 0, 2, 2)


def left_factor(own_ref, ref):
    blocks, rows, span = own_ref.shape
    width = span // 2
    for n in range(blocks):
        lanes = slice(n * span, (n + 1) * span)
        for top, part in zip((0, 2 * rows), halves(own_ref[n])):
            ref[top : top + rows, lanes] = part
            ref[top + rows : top + 2 * rows, lanes] = jnp.concatenate(
                [part[:, width:], -part[:, :width]], axis=1
            )


def right_factor(other_ref, ref):
    blocks, rows, span = other_ref.shape
    for n in range(blocks):
        for top, part in zip((0, rows), halves(other_ref[n])):
            ref[top : top + rows, n * span : (n + 1) * span] = part


def product(left, right):
    rows = left.shape[0] // 4
    mul = lambda a, b: lax.dot_general(a, b, (NT, ((), ())), preferred_element_type=F32)
    high = left[:rows, :] if right is None else right[:rows, :]
    low = left[2 * rows : 3 * rows, :] if right is None else right[rows:, :]
    both = mul(left[...], high)
    return both[: 2 * rows] + both[2 * rows :] + mul(left[: 2 * rows, :], low)


def own_kernel(own_ref, o_ref, left):
    left_factor(own_ref, left)
    o_ref[...] = product(left, None)


def middle_kernel(own_ref, other_ref, edge_ref, here_ref, there_ref, left, right):
    left_factor(own_ref, left)
    right_factor(other_ref, right)
    there_ref[...] = product(left, right)
    left_factor(edge_ref, left)
    here_ref[...] = product(left, None)


def last_kernel(place_ref, own_ref, other_ref, before_ref, here_ref, there_ref, o_ref, left, right):
    left_factor(own_ref, left)
    right_factor(other_ref, right)
    there = there_ref[...] + product(left, right)
    rows = here_ref.shape[1]
    group = rows // Y
    for y in range(Y):
        x, turn = handed_to(y, place_ref[0])
        for part in range(2):
            start = part * rows + y * group
            here = slice(start, start + group)
            o_ref[x, turn, part, :, :rows] = before_ref[here, :] + here_ref[here, :]
            o_ref[x, turn, part, :, rows:] = there[start : start + group]


def handed_to(y, at_y):
    ahead = lax.rem(y - at_y + Y, Y)
    pair = lax.div(lax.rem(ahead + 1, Y), 2)
    x = lax.rem(at_y + 2 - pair + X, X)
    turn = lax.rem(ahead + 1 + lax.div(at_y, X), 2)
    return x, turn


def last_sends():
    sends = [[], []]
    for at_y in range(Y):
        for y in range(Y):
            ahead = (y - at_y) % Y
            x = (at_y + 2 - (ahead + 1) % Y // 2) % X
            turn = (ahead + 1 + at_y // X) % 2
            sends[turn].append((at_y * X + x, y * X + at_y % X))
    return sends


def call(kernel, out_shape, scratch, flops, moved, name, *operands, place=None):
    scalars = [] if place is None else [place]
    return pl.pallas_call(
        kernel,
        out_shape=out_shape,
        in_specs=[SMEM] * len(scalars) + [VMEM] * len(operands),
        out_specs=jax.tree.map(lambda _: VMEM, out_shape),
        scratch_shapes=scratch,
        compiler_params=params(12),
        cost_estimate=cost(flops, moved),
        name=name,
    )(*scalars, *operands)


def sum_kernel(scale, parts_ref, first_ref, second_ref):
    for turn, out in enumerate((first_ref, second_ref)):
        total = parts_ref[0, turn]
        for x in range(1, X):
            total = total + parts_ref[x, turn]
        out[...] = total * scale


def place_kernel(swap_ref, side_ref, first_ref, second_ref, o_ref):
    swap, side = swap_ref[0], side_ref[0]
    rows = o_ref.shape[3] // 2
    group = rows // Y
    tile = 4 * group
    lane = lax.broadcasted_iota(jnp.int32, (o_ref.shape[2], tile), 1)
    odd, late = (lane & group) != 0, lane >= 2 * group
    for source, place in ((first_ref, swap), (second_ref, 1 - swap)):
        for part in range(2):
            own, other = source[part, :, :rows], source[part, :, rows:]
            low, high = jnp.where(side == 0, own, other), jnp.where(side == 0, other, own)
            for y in range(0, Y, 2):
                here = slice(y * group // tile * tile, y * group // tile * tile + tile)
                ahead = y * group % tile
                turned = [
                    pltpu.roll(values[:, here], (n * group - ahead - n // 2 * group) % tile, 1)
                    for n, values in enumerate((low, high, low, high))
                ]
                pair = [jnp.where(odd, turned[n + 1], turned[n]) for n in (0, 2)]
                o_ref[part, place, :, 2 * y * group : 2 * y * group + tile] = jnp.where(late, pair[1], pair[0])


def border_kernel(x_ref, low_ref, high_ref, sems):
    count = low_ref.shape[0]
    half = count // 2
    copies = []
    for start, out in ((x_ref.shape[0] - count, high_ref), (0, low_ref)):
        for part in range(2):
            source = x_ref.at[pl.ds(start + part * half, half)]
            copies.append(pltpu.make_async_copy(source, out.at[pl.ds(part * half, half)], sems.at[len(copies)]))
            copies[-1].start()
    for copy in copies:
        copy.wait()


def per_device(echoes, filter_taps):
    width = echoes.shape[3]
    pulses = echoes.shape[2]
    gate_count = width * X * Z
    at_x, at_y = lax.axis_index("x"), lax.axis_index("y")
    first = (at_x == 0).astype(jnp.int32).reshape(1)
    swapped = (at_y + at_x + 1 & 1).astype(jnp.int32).reshape(1)
    side = lax.axis_index("core").astype(jnp.int32).reshape(1)

    sent = doppler(echoes)
    taps = filter_taps.reshape(2, -1, width)
    rows = 2 * echoes.shape[1]
    got = lax.all_to_all(sent.reshape(pulses, rows, width), ("z", "y"), 0, 0, tiled=True)
    border = jax.ShapeDtypeStruct((2 * Y, rows, width), F32)
    low, high = pl.pallas_call(
        border_kernel,
        out_shape=(border, border),
        in_specs=[VMEM],
        out_specs=(pl.BlockSpec(memory_space=pltpu.HBM),) * 2,
        scratch_shapes=[pltpu.SemaphoreType.DMA((4,))],
        compiler_params=params(2),
        cost_estimate=cost(1e4, 2e6),
        name="borders",
    )(got)
    before = lax.ppermute(high, "x", [(i, (i + 1) % X) for i in range(X)])
    after = lax.ppermute(low, "x", [(i, i - 1) for i in range(1, X)])

    channels = Y * rows // 2
    span = 2 * width
    block = jax.ShapeDtypeStruct((4, channels, span), F32)
    one = 6 * channels * span * span
    inner, outer = pl.pallas_call(
        filter_kernel,
        out_shape=(block, block),
        in_specs=[VMEM] * 2,
        out_specs=(pl.BlockSpec(memory_space=pltpu.HBM), VMEM),
        scratch_shapes=[pltpu.VMEM((channels, Z * span), BF16)] * 2
        + [pltpu.VMEM(((taps.shape[1] + 1) * span, span), BF16)] * 2
        + [pltpu.VMEM(block.shape, F32), pltpu.SemaphoreType.DMA((4,))],
        compiler_params=params(10),
        cost_estimate=cost(34 * one, 6e6),
        name="filter_inner",
    )(got, taps)
    swap = [(0, 1), (1, 0)]
    inner_other = lax.ppermute(inner, "core", swap)
    depth = 4 * span
    left = pltpu.VMEM((4 * channels, depth), BF16)
    right = pltpu.VMEM((2 * channels, depth), BF16)
    square = jax.ShapeDtypeStruct((2 * channels, channels), F32)
    unit = 6 * 2 * channels * channels * depth
    here = call(own_kernel, square, [left], unit, 3e6, "own_inner", inner)
    outer, here = lax.optimization_barrier((outer, here))
    edge = pl.pallas_call(
        edge_kernel,
        out_shape=block,
        in_specs=[SMEM] + [pl.BlockSpec(memory_space=pltpu.HBM)] * 2 + [VMEM] * 2,
        out_specs=VMEM,
        scratch_shapes=[pltpu.VMEM((channels, 2 * span), BF16)] * 4
        + [pltpu.VMEM((4 * span, span), BF16)] * 2
        + [pltpu.VMEM((2,) + border.shape, F32), pltpu.SemaphoreType.DMA((2,))],
        compiler_params=params(10),
        cost_estimate=cost(6 * one, 4e6),
        name="filter_edge",
    )(first, before, after, outer, taps)
    edge_other = lax.ppermute(edge, "core", swap)
    here_edge, there = call(
        middle_kernel, (square, square), [left, right], 2 * unit, 6e6, "other_inner", inner, inner_other, edge
    )
    group = channels // Y
    spread = jax.ShapeDtypeStruct((X, 2, 2, group, 2 * channels), F32)
    total = call(
        last_kernel, spread, [left, right], unit, 5e6, "other_edge", edge, edge_other, here, here_edge, there,
        place=at_y.astype(jnp.int32).reshape(1),
    )

    parts = lax.all_to_all(total, "x", 0, 0, tiled=True)
    piece = jax.ShapeDtypeStruct((2, group, 2 * channels), F32)
    sends = pl.pallas_call(
        functools.partial(sum_kernel, 1.0 / gate_count),
        out_shape=(piece, piece),
        in_specs=[VMEM],
        out_specs=(VMEM, VMEM),
        compiler_params=params(4),
        cost_estimate=cost(1e6, 2e6),
        name="add_up",
    )(parts)
    got = [lax.ppermute(part, ("y", "x"), pairs) for part, pairs in zip(sends, last_sends())]
    return pl.pallas_call(
        place_kernel,
        out_shape=jax.ShapeDtypeStruct((2, 2, group, 2 * channels), F32),
        in_specs=[SMEM, SMEM, VMEM, VMEM],
        out_specs=VMEM,
        compiler_params=params(4),
        cost_estimate=cost(1e5, 1e6),
        name="place",
    )(swapped, side, *got)


def solution(mesh):
    split = Mesh(mesh.devices.reshape(Y, CORE, X, Z), ("y", "core", "x", "z"))
    in_specs = (P(None, ("y", "core"), None, ("x", "z")), P())
    out_specs = P(None, ("x", "z"), ("y", "core"), None)
    return jax.shard_map(
        per_device, mesh=split, in_specs=in_specs, out_specs=out_specs, check_vma=False
    )
```
